512 devices in a mesh: gx: 16 (over z), gy: 8 (over y_hi, x), gz: 4 (over y_lo, core).
Axes of the slice: x: 4, y: 4 (y_hi: 2, y_lo: 2; y = y_hi * 2 + y_lo), z: 16, core: 2. Of those that a mesh axis runs over, the one named last changes fastest.
Arguments:
- features: bfloat16 [128, 64, 16, 256], P('gx', 'gy', 'gz'), may hold values from -64 to 64
- occupancy: int32 [16, 8, 16], P(None, 'gy', 'gz'), may hold values from 0 to 1, as said below
- norm_gain: float32 [2, 32], replicated, may hold values from 0.1 to 1.9
- norm_shift: float32 [2, 32], replicated, may hold values from -3 to 3
- conv_weight: bfloat16 [2, 32, 864], replicated, may hold values from -0.21875 to 0.21875
- conv_bias: float32 [2, 32], replicated, may hold values from -3 to 3
- qkv_weight: bfloat16 [3, 1024, 1024], P(None, 'gx'), may hold values from -1 to 1
Outputs:
- fine_out: bfloat16 [128, 64, 16, 256], P('gx', 'gy', 'gz')
- attention: bfloat16 [32, 1024, 1024], P(('gy', 'gz'), 'gx')
The draws below stay inside these ranges and needn't reach their ends.
Inputs may be any that keep to these rules, and one draw needn't show every extreme that they name: `occupancy`: each aligned block of 4 bricks along the third dimension holds at least one occupied brick.
All inputs are finite; a program needn't handle non-finite values.
Results may differ from the reference program's by a relative error of at most 0.015.
The reference program's roundings to bfloat16 on the way count: a program that leaves them out, or rounds other values in their place, can miss the bound.
Values may be sent and summed in bfloat16 or wider, within the bound.
A program may use at most 64 MiB of HBM per device.

```python
import jax
import jax.numpy as jnp
from jax import lax

C = 32
GROUPS_NORM = 8
HEADS = 16
RZ = 32
D = 1024
HD = 64
RZ_BRICKS = 4
SEQ = 1024
GROUPS = 32
NX = 128
NY = 64
NZ = 128
NBZ = 16
N_GX = 16
N_GY = 8
N_GZ = 4


def brick_layout(key):
    base_key = jax.random.fold_in(key, 7)
    subkeys = jax.random.split(base_key, 3)
    density = jax.random.randint(subkeys[0], (N_GX, N_GY, N_GZ, 1), 10, 96)
    rolled = jax.random.randint(subkeys[1], (N_GX, N_GY, N_GZ, RZ_BRICKS), 0, 100)
    forced = jax.random.randint(subkeys[2], (N_GX, N_GY, N_GZ, 1), 0, RZ_BRICKS)
    slot_index = lax.broadcasted_iota(jnp.int32, (N_GX, N_GY, N_GZ, RZ_BRICKS), 3)
    occupied = jnp.logical_or(rolled < density, slot_index == forced).astype(jnp.int32)
    return occupied.reshape(N_GX, N_GY, NBZ)


def draw_occupancy(key, part):
    return brick_layout(key)


def draw_features(key, part):
    subkeys = jax.random.split(jax.random.fold_in(key, 11), 3)
    shape = (C, NX, NY, NZ)
    noise_field = jax.random.truncated_normal(subkeys[0], -4.0, 4.0, shape, jnp.float32)
    channel_scale = jnp.exp(jax.random.uniform(subkeys[1], (C,), jnp.float32, jnp.log(0.5), jnp.log(2.0)))
    brick_scale = jnp.exp(jax.random.uniform(subkeys[2], (N_GX, N_GY, NBZ), jnp.float32, jnp.log(0.5), jnp.log(2.0)))
    brick_voxels = jnp.repeat(jnp.repeat(jnp.repeat(brick_scale, 8, axis=0), 8, axis=1), 8, axis=2)
    index_x = lax.broadcasted_iota(jnp.int32, (NX, NY, NZ), 0)
    index_y = lax.broadcasted_iota(jnp.int32, (NX, NY, NZ), 1)
    index_z = lax.broadcasted_iota(jnp.int32, (NX, NY, NZ), 2)
    ramp_factor = 1.0 + 2.0 * (index_x.astype(jnp.float32) / NX + index_y.astype(jnp.float32) / NY + index_z.astype(jnp.float32) / NZ) / 3.0
    values = noise_field * channel_scale[:, None, None, None] * (brick_voxels * ramp_factor)[None]
    return values.reshape(C, NX, NY, NBZ, 8).transpose(1, 2, 3, 0, 4).reshape(NX, NY, NBZ, C * 8).astype(jnp.bfloat16)


def draw_qkv_weight(key, part):
    subkeys = jax.random.split(jax.random.fold_in(key, 23), 1)
    weight = jax.random.truncated_normal(subkeys[0], -6.0, 6.0, (3, D, D), jnp.float32) * D ** (-0.5)
    return weight.astype(jnp.bfloat16)


def normal_values(key, dims, deviation, reach, dtype=jnp.bfloat16):
    return jnp.clip(deviation * jax.random.normal(key, dims, jnp.float32), -reach, reach).astype(dtype)


def setup_inputs(seed: int = 0) -> dict:
    keys = jax.random.split(jax.random.key(seed), 8)
    features = draw_features(jax.random.fold_in(keys[7], 71), 0)
    occupancy = draw_occupancy(jax.random.fold_in(keys[7], 71), 0)
    norm_gain = jnp.clip(1.0 + 0.18 * jax.random.normal(keys[2], (2, C), jnp.float32), 0.1, 1.9)
    norm_shift = normal_values(keys[3], (2, C), 0.5, 3.0, jnp.float32)
    conv_weight = normal_values(keys[4], (2, C, 27 * C), (27 * C) ** -0.5, 0.21875)
    conv_bias = normal_values(keys[5], (2, C), 0.5, 3.0, jnp.float32)
    qkv_weight = draw_qkv_weight(jax.random.fold_in(keys[7], 71), 0)
    return dict(features=features, occupancy=occupancy, norm_gain=norm_gain, norm_shift=norm_shift, conv_weight=conv_weight, conv_bias=conv_bias, qkv_weight=qkv_weight)


EPS = 1e-05

def expand_mask(occupancy):
    brick_grid = jnp.repeat(jnp.repeat(jnp.repeat(occupancy, 8, axis=0), 8, axis=1), 8, axis=2)
    return brick_grid.astype(jnp.float32)

def to_channels(packed):
    return packed.reshape(NX, NY, NBZ, C, 8).transpose(3, 0, 1, 2, 4).reshape(C, NX, NY, NZ)

def from_channels(field):
    return field.reshape(C, NX, NY, NBZ, 8).transpose(1, 2, 3, 0, 4).reshape(NX, NY, NBZ, C * 8)

def activate(values, voxel_mask, gain_row, shift_row):
    group_width = C // GROUPS_NORM
    shaped = values.reshape(GROUPS_NORM, group_width, NX * NY * NZ)
    flat_mask = voxel_mask.reshape(1, 1, NX * NY * NZ)
    counted = jnp.sum(voxel_mask) * group_width
    centre = lax.optimization_barrier(jnp.sum(shaped * flat_mask, axis=(1, 2))) / counted
    centred = (shaped - centre[:, None, None]) * flat_mask
    spread = lax.optimization_barrier(jnp.sum(centred * centred, axis=(1, 2))) / counted
    normed = (shaped - centre[:, None, None]) * lax.rsqrt(spread + EPS)[:, None, None]
    normed = normed.reshape(C, NX * NY * NZ) * gain_row[:, None] + shift_row[:, None]
    return (jax.nn.silu(normed) * flat_mask.reshape(1, -1)).reshape(C, NX, NY, NZ)

def convolve(field, weight):
    padded = jnp.pad(field, ((0, 0), (1, 1), (1, 1), (1, 1)))
    accumulated = jnp.zeros((C, NX * NY * NZ), jnp.float32)
    for shift_x in range(3):
        for shift_y in range(3):
            for shift_z in range(3):
                offset = (shift_x * 3 + shift_y) * 3 + shift_z
                window = padded[:, shift_x:shift_x + NX, shift_y:shift_y + NY, shift_z:shift_z + NZ].reshape(C, NX * NY * NZ)
                accumulated = accumulated + jnp.dot(weight[:, offset * C:(offset + 1) * C], window, preferred_element_type=jnp.float32)
    return accumulated.reshape(C, NX, NY, NZ)

def tokenize(field):
    shaped = field.reshape(C, N_GX, 4, 2, N_GY, 2, 4, N_GZ, RZ // 4, 4)
    moved = shaped.transpose(4, 7, 1, 2, 5, 8, 0, 3, 6, 9)
    return moved.reshape(GROUPS, SEQ, D)

def token_keep(occupancy):
    bricks = occupancy.reshape(N_GX, N_GY, N_GZ, RZ_BRICKS).astype(jnp.float32)
    bricks = jnp.repeat(bricks, 2, axis=3)
    spread_out = jnp.broadcast_to(bricks[:, :, :, None, None, :], (N_GX, N_GY, N_GZ, 4, 2, RZ // 4))
    return spread_out.transpose(1, 2, 0, 3, 4, 5).reshape(GROUPS, SEQ)

def attend(tokens, key_keep, weight):
    flat_weight = weight.reshape(3 * D, D)
    projected = lax.dot_general(tokens, flat_weight, (((1,), (1,)), ((), ())), preferred_element_type=jnp.float32).astype(jnp.bfloat16)
    projected = projected.reshape(SEQ, 3, HEADS, HD)
    queries = projected[:, 0].transpose(1, 0, 2)
    keys_all = projected[:, 1].transpose(1, 0, 2)
    values_all = projected[:, 2].transpose(1, 0, 2)

    def head_out(members):
        head_queries, head_keys, head_values = members
        scores = jnp.dot(head_queries, head_keys.T, preferred_element_type=jnp.float32) * HD ** (-0.5)
        scores = jnp.where(key_keep[None, :] > 0, scores, -jnp.inf)
        row_max = lax.optimization_barrier(jnp.max(scores, axis=1, keepdims=True))
        weights = jnp.exp(scores - row_max)
        totals = lax.optimization_barrier(jnp.sum(weights, axis=1, keepdims=True))
        return jnp.dot(weights.astype(jnp.bfloat16), head_values, preferred_element_type=jnp.float32) / totals
    results = lax.map(head_out, (queries, keys_all, values_all))
    merged = results.transpose(1, 0, 2).reshape(SEQ, D) * key_keep[:, None]
    return merged.astype(jnp.bfloat16)

def reference(features, occupancy, norm_gain, norm_shift, conv_weight, conv_bias, qkv_weight):
    field = to_channels(features)
    voxel_mask = expand_mask(occupancy)
    inputs = field * voxel_mask.astype(jnp.bfloat16)
    first_act = activate(inputs.astype(jnp.float32), voxel_mask, norm_gain[0], norm_shift[0]).astype(jnp.bfloat16)
    middle = (convolve(first_act, conv_weight[0]) + conv_bias[0][:, None, None, None]) * voxel_mask[None]
    second_act = activate(middle, voxel_mask, norm_gain[1], norm_shift[1]).astype(jnp.bfloat16)
    out_field = ((inputs.astype(jnp.float32) + convolve(second_act, conv_weight[1]) + conv_bias[1][:, None, None, None]) * voxel_mask[None]).astype(jnp.bfloat16)
    tokens = tokenize(out_field)
    keeps = token_keep(occupancy)
    attention = lax.map(lambda member: attend(member[0], member[1], qkv_weight), (tokens, keeps))
    return (from_channels(out_field), attention)
```

```python
import functools

import jax
import jax.numpy as jnp
from jax import lax
from jax.experimental import pallas as pl
from jax.experimental.pallas import tpu as pltpu
from jax.sharding import PartitionSpec as P

F32 = jnp.float32
BF16 = jnp.bfloat16
MESH = pl.DeviceIdType.MESH
EPS = 1e-05
EMPTY = 1024.0
FAR = -1e30
PIECES = 4
NT = (((1,), (1,)), ((), ()))
NN = (((1,), (0,)), ((), ()))


def iota(shape, dim):
    return lax.broadcasted_iota(jnp.int32, shape, dim)


def dot(a, b, dims=NN):
    return lax.dot_general(a, b, dims, preferred_element_type=F32)


def exact(a, b):
    return lax.dot_general(a, b, NN, precision=lax.Precision.HIGHEST, preferred_element_type=F32)


def one_hot(cond, dtype=F32):
    return jnp.where(cond, 1.0, 0.0).astype(dtype)


def pack_sums(total, squares, count):
    row, lane = iota((256, 128), 0) // 32, iota((256, 128), 1)
    sums = exact(total, one_hot(row == lane)) + exact(squares, one_hot(row == lane - 8))
    sums = jnp.sum(sums, axis=0, keepdims=True)
    at = iota((1, 128), 1)
    return jnp.where(jnp.logical_and(at >= 16, at < 24), count, sums)


def merge(rows):
    counts = jnp.concatenate([rows[:, 16:], rows[:, :16]], axis=1)
    squares = jnp.concatenate([rows[:, 8:], rows[:, :8]], axis=1)
    live = iota(rows.shape, 1) < 8
    counts = jnp.where(live, counts, 1.0)
    total = jnp.sum(rows, axis=0, keepdims=True)
    count = jnp.sum(counts, axis=0, keepdims=True)
    mean = total / count
    off = rows / counts - mean
    spread = jnp.sum(squares + counts * off * off, axis=0, keepdims=True)
    return total, spread, count


def repack(total, spread, count):
    at = iota((1, 128), 1)
    spread = jnp.concatenate([spread[:, 120:], spread[:, :120]], axis=1)
    count = jnp.concatenate([count[:, 112:], count[:, :112]], axis=1)
    tail = jnp.where(at < 24, count, 0.0)
    return jnp.where(at < 8, total, jnp.where(at < 16, spread, tail))


def lanes_of(total, spread, count):
    live = iota((1, 128), 1) < 8
    mean = jnp.where(live, total / count, 0.0)
    scale = jnp.where(live, lax.rsqrt(spread / count + EPS), 0.0)
    both = jnp.concatenate([jnp.broadcast_to(mean, (8, 128)), jnp.broadcast_to(scale, (8, 128))], axis=0)
    wide = exact(both, one_hot(iota((128, 256), 0) == iota((128, 256), 1) // 32))
    return wide[0:1], wide[8:9]


def activated(values, mask, mean, scale, shift):
    normed = (values - mean) * scale + shift
    return jnp.where(mask, normed / (1.0 + jnp.exp(-normed)), 0.0)


def edges(act):
    lane = iota(act.shape, 2) % 8
    before, after = pltpu.roll(act, 1, 1), pltpu.roll(act, 7, 1)
    return jnp.where(lane == 7, before, jnp.where(lane == 0, after, 0.0))


def kernel(
    n_x, n_y, n_z,
    occ, feat, gain, shift, cw, bias, qkv_in,
    fine, att,
    raw, raw_z, cells, taps, taps_e, mid, taps2, taps2_e, banded, wide, pick,
    weights, qkv_raw, tok_f, tok, q_all, k_all, v_all, ready, heads,
    plane_rows, line_rows,
    plane_send, plane_recv, line_send, line_recv, halo_send, halo_recv,
    right_send, right_recv, left_send, left_recv, out_send, out_recv, load_sem,
):
    gx, gy, gz = lax.axis_index("gx"), lax.axis_index("gy"), lax.axis_index("gz")
    n_plane = n_y * n_z
    plane = gy * n_z + gz

    def plane_peer(d):
        other = lax.rem(plane + d, n_plane)
        return (gx, other // n_z, lax.rem(other, n_z))

    def line_peer(d):
        return (lax.rem(gx + d, n_x), gy, gz)

    barrier = pltpu.get_barrier_semaphore()

    @pl.loop(1, n_x)
    def _(d):
        pl.semaphore_signal(barrier, inc=1, device_id=line_peer(d), device_id_type=MESH)

    @pl.loop(1, n_plane)
    def _(d):
        pl.semaphore_signal(barrier, inc=1, device_id=plane_peer(d), device_id_type=MESH)

    load = pltpu.make_async_copy(qkv_in, qkv_raw, load_sem)
    load.start()

    def remote(src, dst, send, recv, peer):
        return pltpu.make_async_remote_copy(
            src_ref=src, dst_ref=dst, send_sem=send, recv_sem=recv, device_id=peer, device_id_type=MESH
        )

    def plane_copy(turn, d):
        return remote(
            plane_rows.at[turn, 0], plane_rows.at[turn, d], plane_send.at[turn, d], plane_recv.at[turn, d], plane_peer(d)
        )

    def line_copy(turn, d):
        return remote(
            line_rows.at[turn, 0], line_rows.at[turn, d], line_send.at[turn, d], line_recv.at[turn, d], line_peer(d)
        )

    def start_all(copy, turn, count):
        @pl.loop(1, count)
        def _(d):
            copy(turn, d).start()

    def wait_recv_all(copy, turn, count):
        @pl.loop(1, count)
        def _(d):
            copy(turn, d).wait_recv()

    def wait_send_all(copy, turn, count):
        @pl.loop(1, count)
        def _(d):
            copy(turn, d).wait_send()

    keeps = [(occ[gx, b] > 0).astype(F32) for b in range(4)]
    brick = iota((8, 4, 256), 1)
    own_keep = jnp.zeros((8, 4, 256), F32)
    for b in range(4):
        own_keep = jnp.where(brick == b, keeps[b], own_keep)
    count = 2048.0 * (keeps[0] + keeps[1] + keeps[2] + keeps[3])

    def fold(block):
        return jnp.sum(block, axis=0)

    def first_sums(x, acc):
        value = feat[x].astype(F32)
        raw[x + 2, 2:10] = jnp.where(own_keep > 0, value, EMPTY).astype(BF16)
        return acc + fold(value * own_keep)

    total = lax.fori_loop(0, 8, first_sums, jnp.zeros((4, 256), F32))
    same = one_hot(iota((256, 256), 0) // 32 == iota((256, 256), 1) // 32)

    def mean_lanes(total):
        rows = jnp.broadcast_to(jnp.sum(total, axis=0, keepdims=True), (8, 256))
        return exact(rows, same)[0:1] / count

    mean = mean_lanes(total)

    def first_squares(x, acc):
        off = (feat[x].astype(F32) - mean) * own_keep
        return acc + fold(off * off)

    squares = lax.fori_loop(0, 8, first_squares, jnp.zeros((4, 256), F32))

    def as_rows(part):
        return jnp.broadcast_to(jnp.sum(part, axis=0, keepdims=True), (8, 256)) * 0.125

    plane_rows[0, 0] = pack_sums(as_rows(total), as_rows(squares), count)

    def expand(n):
        rows = one_hot(iota((256, 32), 0) // 8 == iota((256, 32), 1), BF16)
        wide[:, 0:864] = dot(rows, cw[n]).astype(BF16)
        z_out, z_in = iota((256, 256), 0) % 8, iota((256, 256), 1) % 8

        @pl.loop(0, 9)
        def _(tap):
            parts = []
            for e in range(3):
                off = tap * 3 + e
                lanes = pl.ds(pl.multiple_of((off // 4) * 128, 128), 128)
                parts.append(dot(wide[:, lanes], pick[lax.rem(off, 4)]))
            low, centre, high = parts
            main = jnp.where(z_in == z_out, centre, 0.0)
            main = jnp.where(z_in - z_out == -1, low, main)
            main = jnp.where(z_in - z_out == 1, high, main)
            edge = jnp.where(jnp.logical_and(z_in == 7, z_out == 0), low, 0.0)
            edge = jnp.where(jnp.logical_and(z_in == 0, z_out == 7), high, edge)
            banded[n, tap] = main.astype(BF16)
            banded[n, 9 + tap] = edge.astype(BF16)

    wide[:, 768:896] = jnp.zeros((256, 128), BF16)
    for r in range(4):
        pick[r] = one_hot(iota((128, 256), 0) - 32 * r == iota((128, 256), 1) // 8, BF16)

    pl.semaphore_wait(barrier, n_x + n_plane - 2)
    start_all(plane_copy, 0, n_plane)

    next_x, last_x = line_peer(1), line_peer(n_x - 1)
    next_y = (gx, lax.rem(gy + 1, n_y), gz)
    last_y = (gx, lax.rem(gy + n_y - 1, n_y), gz)
    next_z = (gx, gy, lax.rem(gz + 1, n_z))
    last_z = (gx, gy, lax.rem(gz + n_z - 1, n_z))

    def halo(k, src, dst, peer):
        return remote(src, dst, halo_send.at[k], halo_recv.at[k], peer)

    halo_x = (
        halo(0, raw.at[8:10, 2:10], raw.at[0:2, 2:10], next_x),
        halo(1, raw.at[2:4, 2:10], raw.at[10:12, 2:10], last_x),
    )
    halo_y = (
        halo(2, raw.at[:, 8:10], raw.at[:, 0:2], next_y),
        halo(3, raw.at[:, 2:4], raw.at[:, 10:12], last_y),
    )
    halo_z = (
        halo(4, raw, raw_z.at[0], next_z),
        halo(5, raw, raw_z.at[1], last_z),
    )
    for copy in halo_x:
        copy.start()

    spread_lanes = one_hot(iota((32, 256), 0) == iota((32, 256), 1) // 8)
    small = jnp.concatenate([gain[...], shift[...], bias[...], jnp.zeros((2, 32), F32)], axis=0)
    by_lane = exact(small, spread_lanes)

    for copy in halo_x:
        copy.wait_recv()
    for copy in halo_y:
        copy.start()
    wait_recv_all(plane_copy, 0, n_plane)
    line_rows[0, 0] = repack(*merge(plane_rows[0].reshape(n_plane, 128)))
    start_all(line_copy, 0, n_x)
    for copy in halo_y:
        copy.wait_recv()
    for copy in halo_z:
        copy.start()
    expand(0)
    for copy in halo_z:
        copy.wait_recv()

    y_at = iota((12, 4, 256), 0)
    y_ok = jnp.logical_and(jnp.logical_or(y_at >= 2, gy > 0), jnp.logical_or(y_at < 10, gy < n_y - 1))

    @pl.loop(0, 12)
    def _(x):
        x_ok = jnp.logical_and(jnp.logical_or(x >= 2, gx > 0), jnp.logical_or(x < 10, gx < n_x - 1))
        ok = jnp.logical_and(y_ok, x_ok)
        own = jnp.where(ok, raw[x].astype(F32), EMPTY)
        before = jnp.where(jnp.logical_and(ok, gz > 0), raw_z[0, x].astype(F32), EMPTY)
        after = jnp.where(jnp.logical_and(ok, gz < n_z - 1), raw_z[1, x].astype(F32), EMPTY)
        cells[x, :, 1:5] = own
        cells[x, :, 0:1] = before[:, 3:4]
        cells[x, :, 5:6] = after[:, 0:1]
        cells[x, :, 6:8] = jnp.full((12, 2, 256), EMPTY, F32)

    wait_recv_all(line_copy, 0, n_x)
    mean, scale = lanes_of(*merge(line_rows[0].reshape(n_x, 128)))
    scale = scale * by_lane[0:1]

    @pl.loop(0, 12)
    def _(x):
        value = cells[x]
        act = activated(value, value < 512.0, mean, scale, by_lane[2:3])
        edge = edges(act)
        taps[x] = jnp.concatenate([act[0:7], act[5:12]], axis=1).astype(BF16)
        taps_e[x] = jnp.concatenate([edge[0:7], edge[5:12]], axis=1).astype(BF16)

    row8 = iota((1, 8, 256), 1)
    inner = jnp.logical_and(row8 >= 1, row8 < 5)

    @pl.loop(0, 5)
    def _(step):
        x = step * 2
        acc = jnp.zeros((160, 256), F32)
        for tap in range(9):
            dx, dy = tap // 3, tap % 3
            at = pl.ds(x + dx, 2)
            acc = acc + dot(taps[at, dy : dy + 5].reshape(160, 256), banded[0, tap], NT)
            acc = acc + dot(taps_e[at, dy : dy + 5].reshape(160, 256), banded[0, 9 + tap], NT)
        acc = (acc + by_lane[4:5]).reshape(2, 5, 16, 256)
        for k in range(2):
            mid[x + k, 0:5] = jnp.where(cells[x + k + 1, 1:6] < 512.0, acc[k, :, 0:8], 0.0)
            mid[x + k, 5:10] = jnp.where(cells[x + k + 1, 6:11] < 512.0, acc[k, :, 8:16], 0.0)

    def second_sums(x, acc):
        return acc + jnp.sum(jnp.where(inner, mid[x + 1, 1:9], 0.0), axis=0)

    total = lax.fori_loop(0, 8, second_sums, jnp.zeros((8, 256), F32))
    mean = mean_lanes(total)

    def second_squares(x, acc):
        keep = jnp.logical_and(inner, cells[x + 2, 2:10] < 512.0)
        off = jnp.where(keep, mid[x + 1, 1:9] - mean, 0.0)
        return acc + jnp.sum(off * off, axis=0)

    squares = lax.fori_loop(0, 8, second_squares, jnp.zeros((8, 256), F32))
    plane_rows[1, 0] = pack_sums(total, squares, count)
    start_all(plane_copy, 1, n_plane)
    expand(1)
    wait_recv_all(plane_copy, 1, n_plane)
    line_rows[1, 0] = repack(*merge(plane_rows[1].reshape(n_plane, 128)))
    start_all(line_copy, 1, n_x)

    load.wait()
    from_f, to_f = iota((1024, 128), 0), iota((1024, 128), 1)
    source = (to_f // 4) * 32 + lax.rem(to_f, 4)

    @pl.loop(0, 8)
    def _(xy):
        move = one_hot(from_f == source + xy * 4, BF16)
        lanes = pl.ds(pl.multiple_of(xy * 128, 128), 128)
        moved = dot(qkv_raw[...].reshape(192, 1024), move)
        for k in range(3):
            weights[k * 128 : k * 128 + 64, lanes] = moved[k * 64 : k * 64 + 64].astype(BF16)
            weights[k * 128 + 64 : k * 128 + 128, lanes] = jnp.zeros((64, 128), BF16)

    wait_recv_all(line_copy, 1, n_x)
    mean, scale = lanes_of(*merge(line_rows[1].reshape(n_x, 128)))
    scale = scale * by_lane[1:2]

    @pl.loop(0, 10)
    def _(x):
        act = activated(mid[x], cells[x + 1, 1:11] < 512.0, mean, scale, by_lane[3:4])
        edge = edges(act)
        taps2[x] = jnp.concatenate([act[0:6], act[4:10]], axis=1).astype(BF16)
        taps2_e[x] = jnp.concatenate([edge[0:6], edge[4:10]], axis=1).astype(BF16)

    lane_in, lane_out = iota((256, 256), 0), iota((256, 256), 1)
    wanted = (lax.rem(lane_out, 128) // 4) * 8 + (lane_out // 128) * 4 + lax.rem(lane_out, 4)
    split = one_hot(lane_in == wanted, BF16)
    lower = iota((8, 256), 0) < 4

    @pl.loop(0, 4)
    def _(step):
        x = step * 2
        acc = jnp.zeros((128, 256), F32)
        for tap in range(9):
            dx, dy = tap // 3, tap % 3
            at = pl.ds(x + dx, 2)
            acc = acc + dot(taps2[at, dy : dy + 4].reshape(128, 256), banded[1, tap], NT)
            acc = acc + dot(taps2_e[at, dy : dy + 4].reshape(128, 256), banded[1, 9 + tap], NT)
        acc = (acc + by_lane[5:6]).reshape(2, 4, 16, 256)
        rows = []
        for k in range(2):
            value = jnp.concatenate([cells[x + k + 2, 2:6], cells[x + k + 2, 6:10]], axis=1)
            result = jnp.where(value < 512.0, value + acc[k], 0.0)
            fine[x + k, 0:4] = result[:, 1:5].astype(BF16)
            fine[x + k, 4:8] = result[:, 9:13].astype(BF16)
            rows.append(result.astype(BF16).reshape(64, 256))
        moved = dot(jnp.concatenate(rows, axis=0), split).reshape(2, 4, 16, 256)
        for k in range(2):
            for y in range(4):
                low, high = moved[k, y, 0:8], moved[k, y, 8:16]
                tile = jnp.where(lower, pltpu.roll(low, 7, 0), pltpu.roll(high, 3, 0))
                lanes = slice((k * 4 + y) * 128, (k * 4 + y + 1) * 128)
                tok_f[0, step, :, lanes] = tile[:, 0:128]
                tok_f[1, step, :, lanes] = tile[:, 128:256]

    tok[gx] = tok_f[...].reshape(64, 1024).astype(BF16)

    steps_right, steps_left = n_x // 2, n_x - 1 - n_x // 2
    rows_each = 64 // PIECES
    right, left = line_peer(1), line_peer(n_x - 1)

    def piece(block, c):
        return tok.at[block, pl.ds(c * rows_each, rows_each)]

    def go_right(k, c):
        block = lax.rem(gx - k + n_x, n_x)
        return remote(piece(block, c), piece(block, c), right_send.at[k, c], right_recv.at[k, c], right)

    def go_left(k, c):
        block = lax.rem(gx + k, n_x)
        return remote(piece(block, c), piece(block, c), left_send.at[k, c], left_recv.at[k, c], left)

    lane = iota((64, 128), 1)
    brick_row = lax.rem(iota((64, 128), 0), 4)

    def project(block):
        out = dot(tok[block], weights[...], NT)
        at = pl.ds(pl.multiple_of(block * 64, 64), 64)
        far = jnp.zeros((64, 128), F32)
        for b in range(4):
            keep = (occ[block, b] > 0).astype(F32)
            far = jnp.where(brick_row == b, (1.0 - keep) * FAR, far)
        q_all[at] = jnp.where(lane == 64, 1.0, out[:, 0:128].astype(BF16).astype(F32) * 0.125).astype(BF16)
        k_all[at] = jnp.where(lane == 64, far, out[:, 128:256]).astype(BF16)
        v_all[at] = jnp.where(lane == 64, 1.0, out[:, 256:384]).astype(BF16)

    for c in range(PIECES):
        go_right(0, c).start()
        go_left(0, c).start()
    project(gx)

    @pl.loop(1, steps_right)
    def _(k):
        for c in range(PIECES):
            go_right(k - 1, c).wait_recv()
            go_right(k, c).start()
            go_left(k - 1, c).wait_recv()

            @pl.when(k < steps_left)
            def _():
                go_left(k, c).start()

        project(lax.rem(gx - k + n_x, n_x))
        project(lax.rem(gx + k, n_x))

    for c in range(PIECES):
        go_right(steps_right - 1, c).wait_recv()
    project(lax.rem(gx - steps_right + n_x, n_x))

    def attend(first, second):
        at = [pl.ds(pl.multiple_of(m * 64, 64), 64) for m in (first, second)]
        queries = jnp.concatenate([q_all[at[0]], q_all[at[1]]], axis=0)
        scores = dot(queries, k_all[...], NT)
        probs = jnp.exp(scores - jnp.max(scores, axis=1, keepdims=True))
        mixed = dot(probs.astype(BF16), v_all[...])
        result = (mixed / mixed[:, 64:65]).reshape(4, 32, 128)
        low = iota((32, 128), 1) < 64
        for j, m in enumerate((first, second)):
            top, bottom = result[2 * j], result[2 * j + 1]
            ready[m] = jnp.where(low, top, pltpu.roll(bottom, 64, 1)).astype(BF16)

    def out_copy(d):
        m = lax.rem(gx + d, n_x)
        return remote(ready.at[m], heads.at[gx], out_send.at[d], out_recv.at[gx], line_peer(d))

    half = n_x // 2

    @pl.loop(0, half)
    def _(k):
        first, second = half + k, half - 1 - k
        attend(lax.rem(gx + first, n_x), lax.rem(gx + second, n_x))
        out_copy(first).start()

        @pl.when(second > 0)
        def _():
            out_copy(second).start()

    heads[gx] = ready[gx]

    @pl.loop(1, n_x)
    def _(d):
        m = lax.rem(gx + d, n_x)
        remote(ready.at[m], heads.at[m], out_send.at[d], out_recv.at[m], line_peer(d)).wait_recv()

    low = iota((32, 128), 1) < 64
    tops, bottoms = [], []
    for t in range(n_x // 2):
        even, odd = heads[2 * t].astype(F32), heads[2 * t + 1].astype(F32)
        tops.append(jnp.where(low, even, pltpu.roll(odd, 64, 1)))
        bottoms.append(jnp.where(low, pltpu.roll(even, 64, 1), odd))
    stacked = jnp.concatenate([jnp.concatenate(tops, axis=1), jnp.concatenate(bottoms, axis=1)], axis=0)
    row, col = iota((64, 64), 0), iota((64, 64), 1)
    order = one_hot(lax.rem(row, 2) * 32 + row // 2 == col, BF16)
    placed = dot(order, stacked.astype(BF16))
    row = lax.rem(iota(placed.shape, 0) // 2, 4)
    keep_rows = jnp.zeros(placed.shape, F32)
    for b in range(4):
        keep_rows = jnp.where(row == b, keeps[b], keep_rows)
    att[...] = (placed * keep_rows).astype(BF16)

    for turn in range(2):
        wait_send_all(plane_copy, turn, n_plane)
        wait_send_all(line_copy, turn, n_x)
    for copy in halo_x + halo_y + halo_z:
        copy.wait_send()

    @pl.loop(0, steps_right)
    def _(k):
        for c in range(PIECES):
            go_right(k, c).wait_send()

    @pl.loop(0, steps_left)
    def _(k):
        for c in range(PIECES):
            go_left(k, c).wait_send()

    @pl.loop(1, n_x)
    def _(d):
        out_copy(d).wait_send()


def body(n_x, n_y, n_z, features, occupancy, norm_gain, norm_shift, conv_weight, conv_bias, qkv_weight):
    vmem = pl.BlockSpec(memory_space=pltpu.VMEM)
    smem = pl.BlockSpec(memory_space=pltpu.SMEM)
    dma = pltpu.SemaphoreType.DMA
    n_plane = n_y * n_z
    half = n_x // 2
    fine, att = pl.pallas_call(
        functools.partial(kernel, n_x, n_y, n_z),
        out_shape=(
            jax.ShapeDtypeStruct((8, 8, 4, 256), BF16),
            jax.ShapeDtypeStruct((64, 1024), BF16),
        ),
        in_specs=[smem, vmem, vmem, vmem, vmem, vmem, pl.BlockSpec(memory_space=pl.ANY)],
        out_specs=(vmem, vmem),
        scratch_shapes=[
            pltpu.VMEM((12, 12, 4, 256), BF16),
            pltpu.VMEM((2, 12, 12, 4, 256), BF16),
            pltpu.VMEM((12, 12, 8, 256), F32),
            pltpu.VMEM((12, 7, 16, 256), BF16),
            pltpu.VMEM((12, 7, 16, 256), BF16),
            pltpu.VMEM((10, 10, 8, 256), F32),
            pltpu.VMEM((10, 6, 16, 256), BF16),
            pltpu.VMEM((10, 6, 16, 256), BF16),
            pltpu.VMEM((2, 18, 256, 256), BF16),
            pltpu.VMEM((256, 896), BF16),
            pltpu.VMEM((4, 128, 256), BF16),
            pltpu.VMEM((384, 1024), BF16),
            pltpu.VMEM((3, 64, 1024), BF16),
            pltpu.VMEM((2, 4, 8, 1024), F32),
            pltpu.VMEM((n_x, 64, 1024), BF16),
            pltpu.VMEM((n_x * 64, 128), BF16),
            pltpu.VMEM((n_x * 64, 128), BF16),
            pltpu.VMEM((n_x * 64, 128), BF16),
            pltpu.VMEM((n_x, 32, 128), BF16),
            pltpu.VMEM((n_x, 32, 128), BF16),
            pltpu.VMEM((2, n_plane, 1, 128), F32),
            pltpu.VMEM((2, n_x, 1, 128), F32),
            dma((2, n_plane)), dma((2, n_plane)), dma((2, n_x)), dma((2, n_x)),
            dma((6,)), dma((6,)),
            dma((half, PIECES)), dma((half, PIECES)), dma((half, PIECES)), dma((half, PIECES)),
            dma((n_x,)), dma((n_x,)), dma,
        ],
        compiler_params=pltpu.CompilerParams(
            collective_id=0, has_side_effects=True, vmem_limit_bytes=50 * 1024 * 1024
        ),
    )(occupancy[:, 0, :], features, norm_gain, norm_shift, conv_weight, conv_bias, qkv_weight)
    return fine, att[None]


def solution(mesh):
    in_specs = (P("gx", "gy", "gz", None), P(None, "gy", "gz"), P(), P(), P(), P(), P(None, "gx", None))
    out_specs = (P("gx", "gy", "gz", None), P(("gy", "gz"), "gx", None))
    sizes = tuple(mesh.shape[a] for a in ("gx", "gy", "gz"))
    return jax.shard_map(
        functools.partial(body, *sizes), mesh=mesh, in_specs=in_specs, out_specs=out_specs, check_vma=False
    )
```

```python
import functools

import jax
import jax.numpy as jnp
from jax import lax
from jax.experimental import pallas as pl
from jax.experimental.pallas import tpu as pltpu
from jax.sharding import PartitionSpec as P

F32 = jnp.float32
BF16 = jnp.bfloat16
MESH = pl.DeviceIdType.MESH
EPS = 1e-05
EMPTY = 1024.0
FAR = -1e30
PIECES = 4
NT = (((1,), (1,)), ((), ()))
NN = (((1,), (0,)), ((), ()))


def iota(shape, dim):
    return lax.broadcasted_iota(jnp.int32, shape, dim)


def dot(a, b, dims=NN):
    return lax.dot_general(a, b, dims, preferred_element_type=F32)


def exact(a, b):
    high = a.astype(BF16).astype(F32)
    middle = (a - high).astype(BF16).astype(F32)
    low = a - high - middle
    n = a.shape[0]
    out = dot(jnp.concatenate([high, middle, low, jnp.zeros_like(a)], axis=0).astype(BF16), b)
    return out[0:n] + out[n : 2 * n] + out[2 * n : 3 * n]


def one_hot(cond, dtype=BF16):
    return jnp.where(cond, 1.0, 0.0).astype(dtype)


def group_of(lane, z_major):
    return lax.rem(lane, 32) // 4 if z_major else lane // 32


def pack_sums(total, squares, count, z_major):
    row, lane = group_of(iota((256, 128), 0), z_major), iota((256, 128), 1)
    sums = exact(total, one_hot(row == lane)) + exact(squares, one_hot(row == lane - 8))
    sums = jnp.sum(sums, axis=0, keepdims=True)
    at = iota((1, 128), 1)
    return jnp.where(jnp.logical_and(at >= 16, at < 24), count, sums)


def merge(rows):
    counts = jnp.concatenate([rows[:, 16:], rows[:, :16]], axis=1)
    squares = jnp.concatenate([rows[:, 8:], rows[:, :8]], axis=1)
    live = iota(rows.shape, 1) < 8
    counts = jnp.where(live, counts, 1.0)
    total = jnp.sum(rows, axis=0, keepdims=True)
    count = jnp.sum(counts, axis=0, keepdims=True)
    mean = total / count
    off = rows / counts - mean
    spread = jnp.sum(squares + counts * off * off, axis=0, keepdims=True)
    return total, spread, count


def repack(total, spread, count):
    at = iota((1, 128), 1)
    spread = jnp.concatenate([spread[:, 120:], spread[:, :120]], axis=1)
    count = jnp.concatenate([count[:, 112:], count[:, :112]], axis=1)
    tail = jnp.where(at < 24, count, 0.0)
    return jnp.where(at < 8, total, jnp.where(at < 16, spread, tail))


def lanes_of(total, spread, count):
    live = iota((1, 128), 1) < 8
    mean = jnp.where(live, total / count, 0.0)
    scale = jnp.where(live, lax.rsqrt(spread / count + EPS), 0.0)
    both = jnp.concatenate([jnp.broadcast_to(mean, (8, 128)), jnp.broadcast_to(scale, (8, 128))], axis=0)
    wide = exact(both, one_hot(iota((128, 256), 0) == group_of(iota((128, 256), 1), True)))
    return wide[0:1], wide[8:9]


def activated(values, mask, mean, scale, shift):
    normed = (values - mean) * scale + shift
    return jnp.where(mask, normed / (1.0 + jnp.exp(-normed)), 0.0)


def edges(act):
    lane = iota(act.shape, 2)
    before, after = pltpu.roll(act, 1, 1), pltpu.roll(act, 7, 1)
    return jnp.where(lane >= 224, before, jnp.where(lane < 32, after, 0.0))


def kernel(
    n_x, n_y, n_z,
    occ, feat_in, gain_in, shift_in, cw_in, bias_in, qkv_in,
    fine, att,
    feat, gain, shift, cw, bias,
    raw, ends, ends_in, cells, taps, taps_e, mid, taps2, taps2_e, banded, flat,
    weights, qkv_raw, tok_f, tok, q_all, k_all, v_all, ready, heads,
    plane_rows, line_rows,
    plane_send, plane_recv, line_send, line_recv, halo_send, halo_recv,
    right_send, right_recv, left_send, left_recv, out_send, out_recv, load_sem,
):
    gx, gy, gz = lax.axis_index("gx"), lax.axis_index("gy"), lax.axis_index("gz")
    n_plane = n_y * n_z
    plane = gy * n_z + gz

    def plane_peer(d):
        other = lax.rem(plane + d, n_plane)
        return (gx, other // n_z, lax.rem(other, n_z))

    def line_peer(d):
        return (lax.rem(gx + d, n_x), gy, gz)

    pairs = (
        (feat_in, feat), (cw_in, cw), (gain_in, gain), (shift_in, shift), (bias_in, bias), (qkv_in, qkv_raw)
    )
    loads = [pltpu.make_async_copy(a, b, load_sem.at[k]) for k, (a, b) in enumerate(pairs)]
    for load in loads:
        load.start()

    @pl.loop(0, 12)
    def _(x):
        raw[x] = jnp.full((12, 4, 256), EMPTY, BF16)
        ends_in[0, x] = jnp.full((12, 256), EMPTY, BF16)
        ends_in[1, x] = jnp.full((12, 256), EMPTY, BF16)

    barrier = pltpu.get_barrier_semaphore()

    @pl.loop(1, n_x)
    def _(d):
        pl.semaphore_signal(barrier, inc=1, device_id=line_peer(d), device_id_type=MESH)

    @pl.loop(1, n_plane)
    def _(d):
        pl.semaphore_signal(barrier, inc=1, device_id=plane_peer(d), device_id_type=MESH)

    def remote(src, dst, send, recv, peer):
        return pltpu.make_async_remote_copy(
            src_ref=src, dst_ref=dst, send_sem=send, recv_sem=recv, device_id=peer, device_id_type=MESH
        )

    def plane_copy(turn, d):
        return remote(
            plane_rows.at[turn, 0], plane_rows.at[turn, d], plane_send.at[turn, d], plane_recv.at[turn, d], plane_peer(d)
        )

    def line_copy(turn, d):
        return remote(
            line_rows.at[turn, 0], line_rows.at[turn, d], line_send.at[turn, d], line_recv.at[turn, d], line_peer(d)
        )

    def start_all(copy, turn, count):
        @pl.loop(1, count)
        def _(d):
            copy(turn, d).start()

    def wait_recv_all(copy, turn, count):
        @pl.loop(1, count)
        def _(d):
            copy(turn, d).wait_recv()

    def wait_send_all(copy, turn, count):
        @pl.loop(1, count)
        def _(d):
            copy(turn, d).wait_send()

    keeps = [(occ[b, gx] > 0).astype(F32) for b in range(4)]
    brick = iota((8, 4, 256), 1)
    own_keep = jnp.zeros((8, 4, 256), F32)
    for b in range(4):
        own_keep = jnp.where(brick == b, keeps[b], own_keep)
    count = 2048.0 * (keeps[0] + keeps[1] + keeps[2] + keeps[3])
    loads[0].wait()

    def fold(block):
        return jnp.sum(block, axis=0)

    def first_sums(x, acc):
        value = feat[x].astype(F32)
        raw[x + 2, 2:10] = jnp.where(own_keep > 0, value, EMPTY).astype(BF16)
        return acc + fold(value * own_keep)

    total = lax.fori_loop(0, 8, first_sums, jnp.zeros((4, 256), F32))

    def mean_lanes(total, z_major):
        rows = jnp.broadcast_to(jnp.sum(total, axis=0, keepdims=True), (8, 256))
        same = group_of(iota((256, 256), 0), z_major) == group_of(iota((256, 256), 1), z_major)
        return exact(rows, one_hot(same))[0:1] / count

    mean = mean_lanes(total, False)

    def first_squares(x, acc):
        off = (feat[x].astype(F32) - mean) * own_keep
        return acc + fold(off * off)

    squares = lax.fori_loop(0, 8, first_squares, jnp.zeros((4, 256), F32))

    def as_rows(part):
        return jnp.broadcast_to(jnp.sum(part, axis=0, keepdims=True), (8, 256)) * 0.125

    plane_rows[0, 0] = pack_sums(as_rows(total), as_rows(squares), count, False)

    def expand(n):
        flat[:, 0:864] = cw[n].astype(F32)
        whole = flat[...]
        taps_of = [whole[:, 0:128]] + [pltpu.roll(whole, 896 - 96 * t, 1)[:, 0:128] for t in range(1, 9)]
        stacked = jnp.concatenate(taps_of, axis=0).astype(BF16)
        row, lane = iota((128, 256), 0), iota((128, 256), 1)
        same = lax.rem(row, 32) == lax.rem(lane, 32)
        for z in range(8):
            here = jnp.logical_and(same, row // 32 == lane // 32 - z + 1)
            here = jnp.logical_and(here, row < 96)
            moved = dot(stacked, one_hot(here)).astype(BF16)
            banded[n, 0:9, z * 32 : (z + 1) * 32] = moved.reshape(9, 32, 256)
        for z, e, slot in ((0, 0, 7), (7, 2, 0)):
            here = jnp.logical_and(same, jnp.logical_and(row // 32 == e, lane // 32 == slot))
            moved = dot(stacked, one_hot(here)).astype(BF16)
            banded[n, 9:18, z * 32 : (z + 1) * 32] = moved.reshape(9, 32, 256)
        banded[n, 9:18, 32:224] = jnp.zeros((9, 192, 256), BF16)

    flat[:, 768:896] = jnp.zeros((32, 128), F32)

    pl.semaphore_wait(barrier, n_x + n_plane - 2)
    next_x, last_x = line_peer(1), line_peer(n_x - 1)
    next_y = (gx, lax.rem(gy + 1, n_y), gz)
    last_y = (gx, lax.rem(gy + n_y - 1, n_y), gz)
    next_z = (gx, gy, lax.rem(gz + 1, n_z))
    last_z = (gx, gy, lax.rem(gz + n_z - 1, n_z))

    class Halo:
        def __init__(self, k, index, size, up, down):
            self.has_next, self.has_last = index < size - 1, index > 0
            self.up = remote(up[0], up[1], halo_send.at[k], halo_recv.at[k], up[2])
            self.down = remote(down[0], down[1], halo_send.at[k + 1], halo_recv.at[k + 1], down[2])

        def start(self):
            pl.when(self.has_next)(self.up.start)
            pl.when(self.has_last)(self.down.start)

        def wait_recv(self):
            pl.when(self.has_last)(self.up.wait_recv)
            pl.when(self.has_next)(self.down.wait_recv)

        def wait_send(self):
            pl.when(self.has_next)(self.up.wait_send)
            pl.when(self.has_last)(self.down.wait_send)

    halo_x = Halo(
        0, gx, n_x,
        (raw.at[8:10, 2:10], raw.at[0:2, 2:10], next_x),
        (raw.at[2:4, 2:10], raw.at[10:12, 2:10], last_x),
    )
    halo_y = Halo(
        2, gy, n_y,
        (raw.at[:, 8:10], raw.at[:, 0:2], next_y),
        (raw.at[:, 2:4], raw.at[:, 10:12], last_y),
    )
    halo_z = Halo(
        4, gz, n_z,
        (ends.at[0], ends_in.at[0], next_z),
        (ends.at[1], ends_in.at[1], last_z),
    )
    halo_x.start()
    start_all(plane_copy, 0, n_plane)
    for load in loads[1:5]:
        load.wait()
    expand(0)
    halo_x.wait_recv()
    halo_y.start()
    wait_recv_all(plane_copy, 0, n_plane)
    line_rows[0, 0] = repack(*merge(plane_rows[0].reshape(n_plane, 128)))
    start_all(line_copy, 0, n_x)
    spread_lanes = one_hot(iota((32, 256), 0) == lax.rem(iota((32, 256), 1), 32))
    small = jnp.concatenate([gain[...], shift[...], bias[...], jnp.zeros((2, 32), F32)], axis=0)
    by_lane = exact(small, spread_lanes)
    halo_y.wait_recv()

    @pl.loop(0, 12)
    def _(x):
        value = raw[x].astype(F32)
        ends[0, x] = value[:, 3].astype(BF16)
        ends[1, x] = value[:, 0].astype(BF16)
        cells[x, :, 1:5] = value
        cells[x, :, 6:8] = jnp.full((12, 2, 256), EMPTY, F32)

    halo_z.start()
    expand(1)
    halo_z.wait_recv()

    lane_in, lane_out = iota((256, 256), 0), iota((256, 256), 1)
    by_z = one_hot(lane_in == lax.rem(lane_out, 32) * 8 + lane_out // 32)

    @pl.loop(0, 12)
    def _(x):
        cells[x, :, 0] = ends_in[0, x].astype(F32)
        cells[x, :, 5] = ends_in[1, x].astype(F32)
        moved = dot(cells[x].reshape(96, 256).astype(BF16), by_z)
        cells[x] = moved.reshape(12, 8, 256)

    wait_recv_all(line_copy, 0, n_x)
    mean, scale = lanes_of(*merge(line_rows[0].reshape(n_x, 128)))
    scale = scale * by_lane[0:1]

    @pl.loop(0, 12)
    def _(x):
        value = cells[x]
        act = activated(value, value < 512.0, mean, scale, by_lane[2:3])
        edge = edges(act)
        taps[x] = jnp.concatenate([act[0:7], act[5:12]], axis=1).astype(BF16)
        taps_e[x] = jnp.concatenate([edge[0:7], edge[5:12]], axis=1).astype(BF16)

    row8 = iota((1, 8, 256), 1)
    inner = jnp.logical_and(row8 >= 1, row8 < 5)

    @pl.loop(0, 2)
    def _(step):
        x = step * 5
        acc = jnp.zeros((400, 256), F32)
        for tap in range(9):
            dx, dy = tap // 3, tap % 3
            at = pl.ds(x + dx, 5)
            acc = acc + dot(taps[at, dy : dy + 5].reshape(400, 256), banded[0, tap], NT)
            acc = acc + dot(taps_e[at, dy : dy + 5].reshape(400, 256), banded[0, 9 + tap], NT)
        acc = (acc + by_lane[4:5]).reshape(5, 5, 16, 256)
        for k in range(5):
            mid[x + k, 0:5] = jnp.where(cells[x + k + 1, 1:6] < 512.0, acc[k, :, 0:8], 0.0)
            mid[x + k, 5:10] = jnp.where(cells[x + k + 1, 6:11] < 512.0, acc[k, :, 8:16], 0.0)

    def second_sums(x, acc):
        return acc + jnp.sum(jnp.where(inner, mid[x + 1, 1:9], 0.0), axis=0)

    total = lax.fori_loop(0, 8, second_sums, jnp.zeros((8, 256), F32))
    mean = mean_lanes(total, True)

    def second_squares(x, acc):
        keep = jnp.logical_and(inner, cells[x + 2, 2:10] < 512.0)
        off = jnp.where(keep, mid[x + 1, 1:9] - mean, 0.0)
        return acc + jnp.sum(off * off, axis=0)

    squares = lax.fori_loop(0, 8, second_squares, jnp.zeros((8, 256), F32))
    plane_rows[1, 0] = pack_sums(total, squares, count, True)
    start_all(plane_copy, 1, n_plane)
    wait_recv_all(plane_copy, 1, n_plane)
    line_rows[1, 0] = repack(*merge(plane_rows[1].reshape(n_plane, 128)))
    start_all(line_copy, 1, n_x)

    loads[5].wait()
    from_f, to_f = iota((1024, 128), 0), iota((1024, 128), 1)
    source = (to_f // 4) * 32 + lax.rem(to_f, 4)

    @pl.loop(0, 8)
    def _(xy):
        move = one_hot(from_f == source + xy * 4)
        lanes = pl.ds(pl.multiple_of(xy * 128, 128), 128)
        moved = dot(qkv_raw[...].reshape(192, 1024), move)
        for k in range(3):
            weights[k * 128 : k * 128 + 64, lanes] = moved[k * 64 : k * 64 + 64].astype(BF16)
            weights[k * 128 + 64 : k * 128 + 128, lanes] = jnp.zeros((64, 128), BF16)

    wait_recv_all(line_copy, 1, n_x)
    mean, scale = lanes_of(*merge(line_rows[1].reshape(n_x, 128)))
    scale = scale * by_lane[1:2]

    @pl.loop(0, 10)
    def _(x):
        act = activated(mid[x], cells[x + 1, 1:11] < 512.0, mean, scale, by_lane[3:4])
        edge = edges(act)
        taps2[x] = jnp.concatenate([act[0:6], act[4:10]], axis=1).astype(BF16)
        taps2_e[x] = jnp.concatenate([edge[0:6], edge[4:10]], axis=1).astype(BF16)

    wanted = (lane_out // 128 * 4 + lax.rem(lane_out, 4)) * 32 + lax.rem(lane_out, 128) // 4
    split = one_hot(lane_in == wanted)
    by_channel = one_hot(lane_in == lax.rem(lane_out, 8) * 32 + lane_out // 8)
    lower = iota((8, 256), 0) < 4
    steps = n_x // 2
    right, left = line_peer(1), line_peer(n_x - 1)

    def piece(block, c):
        return tok.at[block, pl.ds(c * 16, 16)]

    def go_right(k, c):
        block = lax.rem(gx - k + n_x, n_x)
        return remote(piece(block, c), piece(block, c), right_send.at[k, c], right_recv.at[k, c], right)

    def go_left(k, c):
        block = lax.rem(gx + k, n_x)
        return remote(piece(block, c), piece(block, c), left_send.at[k, c], left_recv.at[k, c], left)

    @pl.loop(0, 2)
    def _(step):
        x = step * 4
        acc = jnp.zeros((256, 256), F32)
        for tap in range(9):
            dx, dy = tap // 3, tap % 3
            at = pl.ds(x + dx, 4)
            acc = acc + dot(taps2[at, dy : dy + 4].reshape(256, 256), banded[1, tap], NT)
            acc = acc + dot(taps2_e[at, dy : dy + 4].reshape(256, 256), banded[1, 9 + tap], NT)
        acc = (acc + by_lane[5:6]).reshape(4, 4, 16, 256)
        rows = []
        for k in range(4):
            value = jnp.concatenate([cells[x + k + 2, 2:6], cells[x + k + 2, 6:10]], axis=1)
            result = jnp.where(value < 512.0, value + acc[k], 0.0)
            rows.append(result.astype(BF16).reshape(64, 256))
        rows = jnp.concatenate(rows, axis=0)
        moved = dot(rows, split).reshape(4, 4, 16, 256)
        for half in range(2):
            for k in range(2):
                for y in range(4):
                    low, high = moved[2 * half + k, y, 0:8], moved[2 * half + k, y, 8:16]
                    tile = jnp.where(lower, pltpu.roll(low, 7, 0), pltpu.roll(high, 3, 0))
                    lanes = slice((k * 4 + y) * 128, (k * 4 + y + 1) * 128)
                    tok_f[half, 0:8, lanes] = tile[:, 0:128]
                    tok_f[half, 8:16, lanes] = tile[:, 128:256]
            c = step * 2 + half
            tok[gx, pl.ds(pl.multiple_of(c * 16, 16), 16)] = tok_f[half].astype(BF16)
            go_right(0, c).start()
            go_left(0, c).start()
        moved = dot(rows, by_channel).reshape(4, 4, 16, 256)
        for k in range(4):
            fine[x + k, 0:4] = moved[k, :, 1:5].astype(BF16)
            fine[x + k, 4:8] = moved[k, :, 9:13].astype(BF16)

    lane = iota((64, 128), 1)
    brick_row = lax.rem(iota((64, 128), 0), 4)

    def project(blocks):
        together = jnp.concatenate([tok[block] for block in blocks], axis=0)
        outs = dot(together, weights[...], NT)
        for j, block in enumerate(blocks):
            out = outs[j * 64 : (j + 1) * 64]
            at = pl.ds(pl.multiple_of(block * 64, 64), 64)
            far = jnp.zeros((64, 128), F32)
            for b in range(4):
                keep = (occ[b, block] > 0).astype(F32)
                far = jnp.where(brick_row == b, (1.0 - keep) * FAR, far)
            q_all[at] = jnp.where(lane == 64, 1.0, out[:, 0:128].astype(BF16).astype(F32) * 0.125).astype(BF16)
            k_all[at] = jnp.where(lane == 64, far, out[:, 128:256]).astype(BF16)
            v_all[at] = jnp.where(lane == 64, 1.0, out[:, 256:384]).astype(BF16)

    project([gx])

    @pl.loop(1, steps)
    def _(k):
        more = k < steps - 1
        for c in range(PIECES):
            go_right(k - 1, c).wait_recv()
            pl.when(jnp.logical_or(more, c < PIECES // 2))(go_right(k, c).start)
            go_left(k - 1, c).wait_recv()
            pl.when(jnp.logical_or(more, c >= PIECES // 2))(go_left(k, c).start)
        project([lax.rem(gx - k + n_x, n_x), lax.rem(gx + k, n_x)])

    for c in range(PIECES):
        if c < PIECES // 2:
            go_right(steps - 1, c).wait_recv()
        else:
            go_left(steps - 1, c).wait_recv()
    project([lax.rem(gx + steps, n_x)])

    def attend(members):
        at = [pl.ds(pl.multiple_of(m * 64, 64), 64) for m in members]
        queries = jnp.concatenate([q_all[a] for a in at], axis=0)
        scores = dot(queries, k_all[...], NT)
        probs = jnp.exp(scores - jnp.max(scores, axis=1, keepdims=True))
        mixed = dot(probs.astype(BF16), v_all[...])
        result = mixed / mixed[:, 64:65]
        low = iota((32, 128), 1) < 64
        for j, m in enumerate(members):
            top, bottom = result[64 * j : 64 * j + 32], result[64 * j + 32 : 64 * j + 64]
            ready[m] = jnp.where(low, top, pltpu.roll(bottom, 64, 1)).astype(BF16)

    def out_copy(d):
        m = lax.rem(gx + d, n_x)
        return remote(ready.at[m], heads.at[gx], out_send.at[d], out_recv.at[gx], line_peer(d))

    @pl.loop(0, n_x // 4)
    def _(k):
        ahead = (steps + 2 * k, steps + 2 * k + 1, steps - 1 - 2 * k, steps - 2 - 2 * k)
        attend([lax.rem(gx + d, n_x) for d in ahead])
        for d in ahead[0:3]:
            out_copy(d).start()
        pl.when(ahead[3] > 0)(out_copy(ahead[3]).start)

    heads[gx] = ready[gx]

    @pl.loop(1, n_x)
    def _(d):
        m = lax.rem(gx + d, n_x)
        remote(ready.at[m], heads.at[m], out_send.at[d], out_recv.at[m], line_peer(d)).wait_recv()

    low = iota((32, 128), 1) < 64
    tops, bottoms = [], []
    for t in range(n_x // 2):
        even, odd = heads[2 * t].astype(F32), heads[2 * t + 1].astype(F32)
        tops.append(jnp.where(low, even, pltpu.roll(odd, 64, 1)))
        bottoms.append(jnp.where(low, pltpu.roll(even, 64, 1), odd))
    stacked = jnp.concatenate([jnp.concatenate(tops, axis=1), jnp.concatenate(bottoms, axis=1)], axis=0)
    row, col = iota((64, 64), 0), iota((64, 64), 1)
    source = row // 16 * 16 + lax.rem(row, 2) * 8 + lax.rem(row, 16) // 8 * 4 + lax.rem(row, 8) // 2
    order = one_hot(source == col)
    placed = dot(order, stacked.astype(BF16))
    row = lax.rem(iota(placed.shape, 0) // 2, 4)
    keep_rows = jnp.zeros(placed.shape, F32)
    for b in range(4):
        keep_rows = jnp.where(row == b, keeps[b], keep_rows)
    att[...] = (placed * keep_rows).astype(BF16)

    for turn in range(2):
        wait_send_all(plane_copy, turn, n_plane)
        wait_send_all(line_copy, turn, n_x)
    for halo in (halo_x, halo_y, halo_z):
        halo.wait_send()

    @pl.loop(0, steps - 1)
    def _(k):
        for c in range(PIECES):
            go_right(k, c).wait_send()
            go_left(k, c).wait_send()

    for c in range(PIECES):
        if c < PIECES // 2:
            go_right(steps - 1, c).wait_send()
        else:
            go_left(steps - 1, c).wait_send()

    @pl.loop(1, n_x)
    def _(d):
        out_copy(d).wait_send()


def body(n_x, n_y, n_z, features, occupancy, norm_gain, norm_shift, conv_weight, conv_bias, qkv_weight):
    vmem = pl.BlockSpec(memory_space=pltpu.VMEM)
    smem = pl.BlockSpec(memory_space=pltpu.SMEM)
    hbm = pl.BlockSpec(memory_space=pltpu.HBM)
    dma = pltpu.SemaphoreType.DMA
    n_plane = n_y * n_z
    half = n_x // 2
    fine, att = pl.pallas_call(
        functools.partial(kernel, n_x, n_y, n_z),
        out_shape=(
            jax.ShapeDtypeStruct((8, 8, 4, 256), BF16),
            jax.ShapeDtypeStruct((64, 1024), BF16),
        ),
        in_specs=[smem] + [hbm] * 6,
        out_specs=(vmem, vmem),
        scratch_shapes=[
            pltpu.VMEM((8, 8, 4, 256), BF16),
            pltpu.VMEM((2, 32), F32),
            pltpu.VMEM((2, 32), F32),
            pltpu.VMEM((2, 32, 864), BF16),
            pltpu.VMEM((2, 32), F32),
            pltpu.VMEM((12, 12, 4, 256), BF16),
            pltpu.VMEM((2, 12, 12, 256), BF16),
            pltpu.VMEM((2, 12, 12, 256), BF16),
            pltpu.VMEM((12, 12, 8, 256), F32),
            pltpu.VMEM((12, 7, 16, 256), BF16),
            pltpu.VMEM((12, 7, 16, 256), BF16),
            pltpu.VMEM((10, 10, 8, 256), F32),
            pltpu.VMEM((10, 6, 16, 256), BF16),
            pltpu.VMEM((10, 6, 16, 256), BF16),
            pltpu.VMEM((2, 18, 256, 256), BF16),
            pltpu.VMEM((32, 896), F32),
            pltpu.VMEM((384, 1024), BF16),
            pltpu.VMEM((3, 64, 1024), BF16),
            pltpu.VMEM((2, 16, 1024), F32),
            pltpu.VMEM((n_x, 64, 1024), BF16),
            pltpu.VMEM((n_x * 64, 128), BF16),
            pltpu.VMEM((n_x * 64, 128), BF16),
            pltpu.VMEM((n_x * 64, 128), BF16),
            pltpu.VMEM((n_x, 32, 128), BF16),
            pltpu.VMEM((n_x, 32, 128), BF16),
            pltpu.VMEM((2, n_plane, 1, 128), F32),
            pltpu.VMEM((2, n_x, 1, 128), F32),
            dma((2, n_plane)), dma((2, n_plane)), dma((2, n_x)), dma((2, n_x)),
            dma((6,)), dma((6,)),
            dma((half, PIECES)), dma((half, PIECES)), dma((half, PIECES)), dma((half, PIECES)),
            dma((n_x,)), dma((n_x,)), dma((6,)),
        ],
        compiler_params=pltpu.CompilerParams(
            collective_id=0, has_side_effects=True, vmem_limit_bytes=50 * 1024 * 1024
        ),
    )(
        *[
            pltpu.with_memory_space_constraint(a, pltpu.HBM)
            for a in (
                jnp.transpose(occupancy, (1, 2, 0))[0],
                features, norm_gain, norm_shift, conv_weight, conv_bias, qkv_weight,
            )
        ]
    )
    return fine, att[None]


def solution(mesh):
    in_specs = (P("gx", "gy", "gz", None), P(None, "gy", "gz"), P(), P(), P(), P(), P(None, "gx", None))
    out_specs = (P("gx", "gy", "gz", None), P(("gy", "gz"), "gx", None))
    sizes = tuple(mesh.shape[a] for a in ("gx", "gy", "gz"))
    return jax.shard_map(
        functools.partial(body, *sizes), mesh=mesh, in_specs=in_specs, out_specs=out_specs, check_vma=False
    )
```

```python
import functools

import jax
import jax.numpy as jnp
from jax import lax
from jax.experimental import pallas as pl
from jax.experimental.pallas import tpu as pltpu
from jax.sharding import PartitionSpec as P

F32 = jnp.float32
BF16 = jnp.bfloat16
MESH = pl.DeviceIdType.MESH
EPS = 1e-05
EMPTY = 1024.0
FAR = -1e30
PIECES = 4
NT = (((1,), (1,)), ((), ()))
NN = (((1,), (0,)), ((), ()))


def iota(shape, dim):
    return lax.broadcasted_iota(jnp.int32, shape, dim)


def dot(a, b, dims=NN):
    return lax.dot_general(a, b, dims, preferred_element_type=F32)


def exact(a, b):
    high = a.astype(BF16).astype(F32)
    middle = (a - high).astype(BF16).astype(F32)
    low = a - high - middle
    n = a.shape[0]
    out = dot(jnp.concatenate([high, middle, low, jnp.zeros_like(a)], axis=0).astype(BF16), b)
    return out[0:n] + out[n : 2 * n] + out[2 * n : 3 * n]


def one_hot(cond, dtype=BF16):
    return jnp.where(cond, 1.0, 0.0).astype(dtype)


def group_of(lane, z_major):
    return (lane & 31) >> 2 if z_major else lane >> 5


def pack_sums(total, squares, count, z_major):
    row, lane = group_of(iota((256, 128), 0), z_major), iota((256, 128), 1)
    sums = exact(total, one_hot(row == lane)) + exact(squares, one_hot(row == lane - 8))
    sums = jnp.sum(sums, axis=0, keepdims=True)
    at = iota((1, 128), 1)
    return jnp.where(jnp.logical_and(at >= 16, at < 24), count, sums)


def merge(rows):
    counts = jnp.concatenate([rows[:, 16:], rows[:, :16]], axis=1)
    squares = jnp.concatenate([rows[:, 8:], rows[:, :8]], axis=1)
    live = iota(rows.shape, 1) < 8
    counts = jnp.where(live, counts, 1.0)
    total = jnp.sum(rows, axis=0, keepdims=True)
    count = jnp.sum(counts, axis=0, keepdims=True)
    mean = total / count
    off = rows / counts - mean
    spread = jnp.sum(squares + counts * off * off, axis=0, keepdims=True)
    return total, spread, count


def repack(total, spread, count):
    at = iota((1, 128), 1)
    spread = jnp.concatenate([spread[:, 120:], spread[:, :120]], axis=1)
    count = jnp.concatenate([count[:, 112:], count[:, :112]], axis=1)
    tail = jnp.where(at < 24, count, 0.0)
    return jnp.where(at < 8, total, jnp.where(at < 16, spread, tail))


def lanes_of(total, spread, count):
    live = iota((1, 128), 1) < 8
    mean = jnp.where(live, total / count, 0.0)
    scale = jnp.where(live, lax.rsqrt(spread / count + EPS), 0.0)
    both = jnp.concatenate([jnp.broadcast_to(mean, (8, 128)), jnp.broadcast_to(scale, (8, 128))], axis=0)
    wide = exact(both, one_hot(iota((128, 256), 0) == group_of(iota((128, 256), 1), True)))
    return wide[0:1], wide[8:9]


def activated(values, mask, mean, scale, shift):
    normed = (values - mean) * scale + shift
    return jnp.where(mask, normed / (1.0 + jnp.exp(-normed)), 0.0)


def edges(act):
    lane = iota(act.shape, 2)
    before, after = pltpu.roll(act, 1, 1), pltpu.roll(act, 7, 1)
    return jnp.where(lane >= 224, before, jnp.where(lane < 32, after, 0.0))


def kernel(
    n_x, n_y, n_z,
    occ, feat_in, gain_in, shift_in, cw_in, bias_in, qkv_in,
    fine, att,
    feat, gain, shift, cw, bias,
    raw, ends, ends_in, cells, taps, taps_e, mid, taps2, taps2_e, banded, flat,
    weights, qkv_raw, results, tok_f, tok, q_all, k_all, v_all, ready, heads,
    plane_rows, line_rows,
    plane_send, plane_recv, line_send, line_recv, halo_send, halo_recv,
    right_send, right_recv, left_send, left_recv, out_send, out_recv, load_sem,
):
    gx, gy, gz = lax.axis_index("gx"), lax.axis_index("gy"), lax.axis_index("gz")
    n_plane = n_y * n_z
    plane = gy * n_z + gz

    def plane_peer(d):
        other = lax.rem(plane + d, n_plane)
        return (gx, lax.div(other, n_z), lax.rem(other, n_z))

    def line_peer(d):
        return (lax.rem(gx + d, n_x), gy, gz)

    barrier = pltpu.get_barrier_semaphore()

    @pl.loop(1, n_x)
    def _(d):
        pl.semaphore_signal(barrier, inc=1, device_id=line_peer(d), device_id_type=MESH)

    @pl.loop(1, n_plane)
    def _(d):
        pl.semaphore_signal(barrier, inc=1, device_id=plane_peer(d), device_id_type=MESH)

    pairs = (
        (feat_in, feat), (cw_in, cw), (gain_in, gain), (shift_in, shift), (bias_in, bias), (qkv_in, qkv_raw)
    )
    loads = [pltpu.make_async_copy(a, b, load_sem.at[k]) for k, (a, b) in enumerate(pairs)]
    for load in loads:
        load.start()

    def empty(ref):
        ref[...] = jnp.full(ref.shape, EMPTY, BF16)

    pl.when(gx == 0)(lambda: empty(raw.at[0:2, 2:10]))
    pl.when(gx == n_x - 1)(lambda: empty(raw.at[10:12, 2:10]))
    pl.when(gy == 0)(lambda: empty(raw.at[:, 0:2]))
    pl.when(gy == n_y - 1)(lambda: empty(raw.at[:, 10:12]))
    pl.when(gz == 0)(lambda: empty(ends_in.at[0]))
    pl.when(gz == n_z - 1)(lambda: empty(ends_in.at[1]))

    def remote(src, dst, send, recv, peer):
        return pltpu.make_async_remote_copy(
            src_ref=src, dst_ref=dst, send_sem=send, recv_sem=recv, device_id=peer, device_id_type=MESH
        )

    def plane_copy(turn, d):
        return remote(
            plane_rows.at[turn, 0], plane_rows.at[turn, d], plane_send.at[turn, d], plane_recv.at[turn, d], plane_peer(d)
        )

    def line_copy(turn, d):
        return remote(
            line_rows.at[turn, 0], line_rows.at[turn, d], line_send.at[turn, d], line_recv.at[turn, d], line_peer(d)
        )

    def start_all(copy, turn, count):
        @pl.loop(1, count)
        def _(d):
            copy(turn, d).start()

    def wait_recv_all(copy, turn, count):
        @pl.loop(1, count)
        def _(d):
            copy(turn, d).wait_recv()

    def wait_send_all(copy, turn, count):
        @pl.loop(1, count)
        def _(d):
            copy(turn, d).wait_send()

    keeps = [(occ[b, gx] > 0).astype(F32) for b in range(4)]
    brick = iota((8, 4, 256), 1)
    own_keep = jnp.zeros((8, 4, 256), F32)
    for b in range(4):
        own_keep = jnp.where(brick == b, keeps[b], own_keep)
    count = 2048.0 * (keeps[0] + keeps[1] + keeps[2] + keeps[3])
    loads[0].wait()

    def fold(block):
        return jnp.sum(block, axis=0)

    def first_sums(x, acc):
        value = feat[x].astype(F32)
        raw[x + 2, 2:10] = jnp.where(own_keep > 0, value, EMPTY).astype(BF16)
        return acc + fold(value * own_keep)

    total = lax.fori_loop(0, 8, first_sums, jnp.zeros((4, 256), F32))

    def mean_lanes(total, z_major):
        rows = jnp.broadcast_to(jnp.sum(total, axis=0, keepdims=True), (8, 256))
        same = group_of(iota((256, 256), 0), z_major) == group_of(iota((256, 256), 1), z_major)
        return exact(rows, one_hot(same))[0:1] / count

    mean = mean_lanes(total, False)

    def first_squares(x, acc):
        off = (feat[x].astype(F32) - mean) * own_keep
        return acc + fold(off * off)

    squares = lax.fori_loop(0, 8, first_squares, jnp.zeros((4, 256), F32))

    def as_rows(part):
        return jnp.broadcast_to(jnp.sum(part, axis=0, keepdims=True), (8, 256)) * 0.125

    plane_rows[0, 0] = pack_sums(as_rows(total), as_rows(squares), count, False)

    def expand(n):
        flat[:, 0:864] = cw[n].astype(F32)
        whole = flat[...]
        taps_of = [whole[:, 0:128]] + [pltpu.roll(whole, 896 - 96 * t, 1)[:, 0:128] for t in range(1, 9)]
        stacked = jnp.concatenate(taps_of, axis=0).astype(BF16)
        row, lane = iota((128, 256), 0), iota((128, 256), 1)
        same = (row & 31) == (lane & 31)
        for z in range(8):
            here = jnp.logical_and(same, (row >> 5) == (lane >> 5) - z + 1)
            here = jnp.logical_and(here, row < 96)
            moved = dot(stacked, one_hot(here)).astype(BF16)
            banded[n, 0:9, z * 32 : (z + 1) * 32] = moved.reshape(9, 32, 256)
        for z, e, slot in ((0, 0, 7), (7, 2, 0)):
            here = jnp.logical_and(same, jnp.logical_and((row >> 5) == e, (lane >> 5) == slot))
            moved = dot(stacked, one_hot(here)).astype(BF16)
            banded[n, 9:18, z * 32 : (z + 1) * 32] = moved.reshape(9, 32, 256)
        banded[n, 9:18, 32:224] = jnp.zeros((9, 192, 256), BF16)

    flat[:, 768:896] = jnp.zeros((32, 128), F32)

    for load in loads[1:5]:
        load.wait()
    expand(0)
    expand(1)
    spread_lanes = one_hot(iota((32, 256), 0) == (iota((32, 256), 1) & 31))
    small = jnp.concatenate([gain[...], shift[...], bias[...], jnp.zeros((2, 32), F32)], axis=0)
    by_lane = exact(small, spread_lanes)
    pl.semaphore_wait(barrier, n_x + n_plane - 2)
    next_x, last_x = line_peer(1), line_peer(n_x - 1)
    next_y = (gx, lax.rem(gy + 1, n_y), gz)
    last_y = (gx, lax.rem(gy + n_y - 1, n_y), gz)
    next_z = (gx, gy, lax.rem(gz + 1, n_z))
    last_z = (gx, gy, lax.rem(gz + n_z - 1, n_z))

    class Halo:
        def __init__(self, k, index, size, up, down):
            self.has_next, self.has_last = index < size - 1, index > 0
            self.up = remote(up[0], up[1], halo_send.at[k], halo_recv.at[k], up[2])
            self.down = remote(down[0], down[1], halo_send.at[k + 1], halo_recv.at[k + 1], down[2])

        def start(self):
            pl.when(self.has_next)(self.up.start)
            pl.when(self.has_last)(self.down.start)

        def wait_recv(self):
            pl.when(self.has_last)(self.up.wait_recv)
            pl.when(self.has_next)(self.down.wait_recv)

        def wait_send(self):
            pl.when(self.has_next)(self.up.wait_send)
            pl.when(self.has_last)(self.down.wait_send)

    halo_x = Halo(
        0, gx, n_x,
        (raw.at[8:10, 2:10], raw.at[0:2, 2:10], next_x),
        (raw.at[2:4, 2:10], raw.at[10:12, 2:10], last_x),
    )
    halo_y = Halo(
        2, gy, n_y,
        (raw.at[:, 8:10], raw.at[:, 0:2], next_y),
        (raw.at[:, 2:4], raw.at[:, 10:12], last_y),
    )
    halo_z = Halo(
        4, gz, n_z,
        (ends.at[0], ends_in.at[0], next_z),
        (ends.at[1], ends_in.at[1], last_z),
    )
    halo_x.start()
    start_all(plane_copy, 0, n_plane)
    halo_x.wait_recv()
    halo_y.start()
    wait_recv_all(plane_copy, 0, n_plane)
    line_rows[0, 0] = repack(*merge(plane_rows[0].reshape(n_plane, 128)))
    start_all(line_copy, 0, n_x)
    halo_y.wait_recv()

    @pl.loop(0, 12)
    def _(x):
        value = raw[x].astype(F32)
        ends[0, x] = value[:, 3].astype(BF16)
        ends[1, x] = value[:, 0].astype(BF16)
        cells[x, :, 1:5] = value
        cells[x, :, 6:8] = jnp.full((12, 2, 256), EMPTY, F32)

    halo_z.start()
    halo_z.wait_recv()

    lane_in, lane_out = iota((256, 256), 0), iota((256, 256), 1)
    by_z = one_hot(lane_in == ((lane_out & 31) << 3) + (lane_out >> 5))

    @pl.loop(0, 12)
    def _(x):
        cells[x, :, 0] = ends_in[0, x].astype(F32)
        cells[x, :, 5] = ends_in[1, x].astype(F32)
        moved = dot(cells[x].reshape(96, 256).astype(BF16), by_z)
        cells[x] = moved.reshape(12, 8, 256)

    wait_recv_all(line_copy, 0, n_x)
    mean, scale = lanes_of(*merge(line_rows[0].reshape(n_x, 128)))
    scale = scale * by_lane[0:1]

    @pl.loop(0, 12)
    def _(x):
        value = cells[x]
        act = activated(value, value < 512.0, mean, scale, by_lane[2:3])
        edge = edges(act)
        taps[x] = jnp.concatenate([act[0:7], act[5:12]], axis=1).astype(BF16)
        taps_e[x] = jnp.concatenate([edge[0:7], edge[5:12]], axis=1).astype(BF16)

    row8 = iota((1, 8, 256), 1)
    inner = jnp.logical_and(row8 >= 1, row8 < 5)

    @pl.loop(0, 1)
    def _(step):
        x = step * 10
        acc = jnp.zeros((800, 256), F32)
        for tap in range(9):
            dx, dy = tap // 3, tap % 3
            at = pl.ds(x + dx, 10)
            acc = acc + dot(taps[at, dy : dy + 5].reshape(800, 256), banded[0, tap], NT)
            acc = acc + dot(taps_e[at, dy : dy + 5].reshape(800, 256), banded[0, 9 + tap], NT)
        acc = (acc + by_lane[4:5]).reshape(10, 5, 16, 256)
        for k in range(10):
            mid[x + k, 0:5] = jnp.where(cells[x + k + 1, 1:6] < 512.0, acc[k, :, 0:8], 0.0)
            mid[x + k, 5:10] = jnp.where(cells[x + k + 1, 6:11] < 512.0, acc[k, :, 8:16], 0.0)

    def second_sums(x, acc):
        return acc + jnp.sum(jnp.where(inner, mid[x + 1, 1:9], 0.0), axis=0)

    total = lax.fori_loop(0, 8, second_sums, jnp.zeros((8, 256), F32))
    mean = mean_lanes(total, True)

    def second_squares(x, acc):
        keep = jnp.logical_and(inner, cells[x + 2, 2:10] < 512.0)
        off = jnp.where(keep, mid[x + 1, 1:9] - mean, 0.0)
        return acc + jnp.sum(off * off, axis=0)

    squares = lax.fori_loop(0, 8, second_squares, jnp.zeros((8, 256), F32))
    plane_rows[1, 0] = pack_sums(total, squares, count, True)
    start_all(plane_copy, 1, n_plane)
    wait_recv_all(plane_copy, 1, n_plane)
    line_rows[1, 0] = repack(*merge(plane_rows[1].reshape(n_plane, 128)))
    start_all(line_copy, 1, n_x)

    loads[5].wait()
    from_f, to_f = iota((1024, 128), 0), iota((1024, 128), 1)
    source = ((to_f >> 2) << 5) + (to_f & 3)

    @pl.loop(0, 8)
    def _(xy):
        move = one_hot(from_f == source + xy * 4)
        lanes = pl.ds(pl.multiple_of(xy * 128, 128), 128)
        moved = dot(qkv_raw[...].reshape(192, 1024), move)
        for k in range(3):
            weights[k * 128 : k * 128 + 64, lanes] = moved[k * 64 : k * 64 + 64].astype(BF16)
            weights[k * 128 + 64 : k * 128 + 128, lanes] = jnp.zeros((64, 128), BF16)

    wait_recv_all(line_copy, 1, n_x)
    mean, scale = lanes_of(*merge(line_rows[1].reshape(n_x, 128)))
    scale = scale * by_lane[1:2]

    @pl.loop(0, 10)
    def _(x):
        act = activated(mid[x], cells[x + 1, 1:11] < 512.0, mean, scale, by_lane[3:4])
        edge = edges(act)
        taps2[x] = jnp.concatenate([act[0:6], act[4:10]], axis=1).astype(BF16)
        taps2_e[x] = jnp.concatenate([edge[0:6], edge[4:10]], axis=1).astype(BF16)

    wanted = ((((lane_out >> 7) << 2) + (lane_out & 3)) << 5) + ((lane_out & 127) >> 2)
    split = one_hot(lane_in == wanted)
    by_channel = one_hot(lane_in == ((lane_out & 7) << 5) + (lane_out >> 3))
    lower = iota((8, 256), 0) < 4
    steps = n_x // 2
    right, left = line_peer(1), line_peer(n_x - 1)

    def piece(block, c):
        return tok.at[block, pl.ds(c * 16, 16)]

    def go_right(k, c):
        block = lax.rem(gx - k + n_x, n_x)
        return remote(piece(block, c), piece(block, c), right_send.at[k, c], right_recv.at[k, c], right)

    def go_left(k, c):
        block = lax.rem(gx + k, n_x)
        return remote(piece(block, c), piece(block, c), left_send.at[k, c], left_recv.at[k, c], left)

    @pl.loop(0, 2)
    def _(step):
        x = step * 4
        acc = jnp.zeros((256, 256), F32)
        for tap in range(9):
            dx, dy = tap // 3, tap % 3
            at = pl.ds(x + dx, 4)
            acc = acc + dot(taps2[at, dy : dy + 4].reshape(256, 256), banded[1, tap], NT)
            acc = acc + dot(taps2_e[at, dy : dy + 4].reshape(256, 256), banded[1, 9 + tap], NT)
        acc = (acc + by_lane[5:6]).reshape(4, 4, 16, 256)
        rows = []
        for k in range(4):
            value = jnp.concatenate([cells[x + k + 2, 2:6], cells[x + k + 2, 6:10]], axis=1)
            result = jnp.where(value < 512.0, value + acc[k], 0.0)
            rows.append(result.astype(BF16).reshape(64, 256))
        rows = jnp.concatenate(rows, axis=0)
        moved = dot(rows, split).reshape(4, 4, 16, 256)
        for half in range(2):
            for k in range(2):
                for y in range(4):
                    low, high = moved[2 * half + k, y, 0:8], moved[2 * half + k, y, 8:16]
                    tile = jnp.where(lower, pltpu.roll(low, 7, 0), pltpu.roll(high, 3, 0))
                    lanes = slice((k * 4 + y) * 128, (k * 4 + y + 1) * 128)
                    tok_f[half, 0:8, lanes] = tile[:, 0:128]
                    tok_f[half, 8:16, lanes] = tile[:, 128:256]
            c = step * 2 + half
            tok[gx, pl.ds(pl.multiple_of(c * 16, 16), 16)] = tok_f[half].astype(BF16)
            go_right(0, c).start()
            go_left(0, c).start()
        results[step] = rows

    lane = iota((64, 128), 1)
    brick_row = iota((64, 128), 0) & 3

    def project(blocks):
        together = jnp.concatenate([tok[block] for block in blocks], axis=0)
        outs = dot(together, weights[...], NT)
        for j, block in enumerate(blocks):
            out = outs[j * 64 : (j + 1) * 64]
            at = pl.ds(pl.multiple_of(block * 64, 64), 64)
            far = jnp.zeros((64, 128), F32)
            for b in range(4):
                keep = (occ[b, block] > 0).astype(F32)
                far = jnp.where(brick_row == b, (1.0 - keep) * FAR, far)
            q_all[at] = jnp.where(lane == 64, 1.0, out[:, 0:128].astype(BF16).astype(F32) * 0.125).astype(BF16)
            k_all[at] = jnp.where(lane == 64, far, out[:, 128:256]).astype(BF16)
            v_all[at] = jnp.where(lane == 64, 1.0, out[:, 256:384]).astype(BF16)

    project([gx])

    @pl.loop(0, 2)
    def _(step):
        moved = dot(results[step], by_channel).reshape(4, 4, 16, 256)
        for k in range(4):
            fine[step * 4 + k, 0:4] = moved[k, :, 1:5].astype(BF16)
            fine[step * 4 + k, 4:8] = moved[k, :, 9:13].astype(BF16)

    @pl.loop(1, steps)
    def _(k):
        more = k < steps - 1
        for c in range(PIECES):
            go_right(k - 1, c).wait_recv()
            pl.when(jnp.logical_or(more, c < PIECES // 2))(go_right(k, c).start)
            go_left(k - 1, c).wait_recv()
            pl.when(jnp.logical_or(more, c >= PIECES // 2))(go_left(k, c).start)
        project([lax.rem(gx - k + n_x, n_x), lax.rem(gx + k, n_x)])

    for c in range(PIECES):
        if c < PIECES // 2:
            go_right(steps - 1, c).wait_recv()
        else:
            go_left(steps - 1, c).wait_recv()
    project([lax.rem(gx + steps, n_x)])

    def attend(members):
        at = [pl.ds(pl.multiple_of(m * 64, 64), 64) for m in members]
        queries = jnp.concatenate([q_all[a] for a in at], axis=0)
        scores = dot(queries, k_all[...], NT)
        probs = jnp.exp(scores - jnp.max(scores, axis=1, keepdims=True))
        mixed = dot(probs.astype(BF16), v_all[...])
        result = mixed / mixed[:, 64:65]
        low = iota((32, 128), 1) < 64
        for j, m in enumerate(members):
            top, bottom = result[64 * j : 64 * j + 32], result[64 * j + 32 : 64 * j + 64]
            ready[m] = jnp.where(low, top, pltpu.roll(bottom, 64, 1)).astype(BF16)

    def out_copy(d):
        m = lax.rem(gx + d, n_x)
        return remote(ready.at[m], heads.at[gx], out_send.at[d], out_recv.at[gx], line_peer(d))

    @pl.loop(0, n_x // 4)
    def _(k):
        ahead = (steps + 2 * k, steps + 2 * k + 1, steps - 1 - 2 * k, steps - 2 - 2 * k)
        attend([lax.rem(gx + d, n_x) for d in ahead])
        for d in ahead[0:3]:
            out_copy(d).start()
        pl.when(ahead[3] > 0)(out_copy(ahead[3]).start)

    heads[gx] = ready[gx]

    @pl.loop(1, n_x)
    def _(d):
        m = lax.rem(gx + d, n_x)
        remote(ready.at[m], heads.at[m], out_send.at[d], out_recv.at[m], line_peer(d)).wait_recv()

    low = iota((32, 128), 1) < 64
    tops, bottoms = [], []
    for t in range(n_x // 2):
        even, odd = heads[2 * t].astype(F32), heads[2 * t + 1].astype(F32)
        tops.append(jnp.where(low, even, pltpu.roll(odd, 64, 1)))
        bottoms.append(jnp.where(low, pltpu.roll(even, 64, 1), odd))
    stacked = jnp.concatenate([jnp.concatenate(tops, axis=1), jnp.concatenate(bottoms, axis=1)], axis=0)
    row, col = iota((64, 64), 0), iota((64, 64), 1)
    source = ((row >> 4) << 4) + ((row & 1) << 3) + (((row & 15) >> 3) << 2) + ((row & 7) >> 1)
    order = one_hot(source == col)
    placed = dot(order, stacked.astype(BF16))
    row = (iota(placed.shape, 0) >> 1) & 3
    keep_rows = jnp.zeros(placed.shape, F32)
    for b in range(4):
        keep_rows = jnp.where(row == b, keeps[b], keep_rows)
    att[...] = (placed * keep_rows).astype(BF16)

    for turn in range(2):
        wait_send_all(plane_copy, turn, n_plane)
        wait_send_all(line_copy, turn, n_x)
    for halo in (halo_x, halo_y, halo_z):
        halo.wait_send()

    @pl.loop(0, steps - 1)
    def _(k):
        for c in range(PIECES):
            go_right(k, c).wait_send()
            go_left(k, c).wait_send()

    for c in range(PIECES):
        if c < PIECES // 2:
            go_right(steps - 1, c).wait_send()
        else:
            go_left(steps - 1, c).wait_send()

    @pl.loop(1, n_x)
    def _(d):
        out_copy(d).wait_send()


def body(n_x, n_y, n_z, features, occupancy, norm_gain, norm_shift, conv_weight, conv_bias, qkv_weight):
    vmem = pl.BlockSpec(memory_space=pltpu.VMEM)
    smem = pl.BlockSpec(memory_space=pltpu.SMEM)
    hbm = pl.BlockSpec(memory_space=pltpu.HBM)
    dma = pltpu.SemaphoreType.DMA
    n_plane = n_y * n_z
    half = n_x // 2
    fine, att = pl.pallas_call(
        functools.partial(kernel, n_x, n_y, n_z),
        out_shape=(
            jax.ShapeDtypeStruct((8, 8, 4, 256), BF16),
            jax.ShapeDtypeStruct((64, 1024), BF16),
        ),
        in_specs=[smem] + [hbm] * 6,
        out_specs=(vmem, vmem),
        scratch_shapes=[
            pltpu.VMEM((8, 8, 4, 256), BF16),
            pltpu.VMEM((2, 32), F32),
            pltpu.VMEM((2, 32), F32),
            pltpu.VMEM((2, 32, 864), BF16),
            pltpu.VMEM((2, 32), F32),
            pltpu.VMEM((12, 12, 4, 256), BF16),
            pltpu.VMEM((2, 12, 12, 256), BF16),
            pltpu.VMEM((2, 12, 12, 256), BF16),
            pltpu.VMEM((12, 12, 8, 256), F32),
            pltpu.VMEM((12, 7, 16, 256), BF16),
            pltpu.VMEM((12, 7, 16, 256), BF16),
            pltpu.VMEM((10, 10, 8, 256), F32),
            pltpu.VMEM((10, 6, 16, 256), BF16),
            pltpu.VMEM((10, 6, 16, 256), BF16),
            pltpu.VMEM((2, 18, 256, 256), BF16),
            pltpu.VMEM((32, 896), F32),
            pltpu.VMEM((384, 1024), BF16),
            pltpu.VMEM((3, 64, 1024), BF16),
            pltpu.VMEM((2, 256, 256), BF16),
            pltpu.VMEM((2, 16, 1024), F32),
            pltpu.VMEM((n_x, 64, 1024), BF16),
            pltpu.VMEM((n_x * 64, 128), BF16),
            pltpu.VMEM((n_x * 64, 128), BF16),
            pltpu.VMEM((n_x * 64, 128), BF16),
            pltpu.VMEM((n_x, 32, 128), BF16),
            pltpu.VMEM((n_x, 32, 128), BF16),
            pltpu.VMEM((2, n_plane, 1, 128), F32),
            pltpu.VMEM((2, n_x, 1, 128), F32),
            dma((2, n_plane)), dma((2, n_plane)), dma((2, n_x)), dma((2, n_x)),
            dma((6,)), dma((6,)),
            dma((half, PIECES)), dma((half, PIECES)), dma((half, PIECES)), dma((half, PIECES)),
            dma((n_x,)), dma((n_x,)), dma((6,)),
        ],
        compiler_params=pltpu.CompilerParams(
            collective_id=0, has_side_effects=True, vmem_limit_bytes=50 * 1024 * 1024
        ),
    )(
        *[
            pltpu.with_memory_space_constraint(a, pltpu.HBM)
            for a in (
                jnp.transpose(occupancy, (1, 2, 0))[0],
                features, norm_gain, norm_shift, conv_weight, conv_bias, qkv_weight,
            )
        ]
    )
    return fine, att[None]


def solution(mesh):
    in_specs = (P("gx", "gy", "gz", None), P(None, "gy", "gz"), P(), P(), P(), P(), P(None, "gx", None))
    out_specs = (P("gx", "gy", "gz", None), P(("gy", "gz"), "gx", None))
    sizes = tuple(mesh.shape[a] for a in ("gx", "gy", "gz"))
    return jax.shard_map(
        functools.partial(body, *sizes), mesh=mesh, in_specs=in_specs, out_specs=out_specs, check_vma=False
    )
```

```python
import functools

import jax
import jax.numpy as jnp
from jax import lax
from jax.experimental import pallas as pl
from jax.experimental.pallas import tpu as pltpu
from jax.sharding import PartitionSpec as P

F32 = jnp.float32
BF16 = jnp.bfloat16
MESH = pl.DeviceIdType.MESH
EPS = 1e-05
EMPTY = 1024.0
FAR = -1e30
PIECES = 4
NT = (((1,), (1,)), ((), ()))
NN = (((1,), (0,)), ((), ()))


def iota(shape, dim):
    return lax.broadcasted_iota(jnp.int32, shape, dim)


def dot(a, b, dims=NN):
    return lax.dot_general(a, b, dims, preferred_element_type=F32)


def exact(a, b):
    high = a.astype(BF16).astype(F32)
    middle = (a - high).astype(BF16).astype(F32)
    low = a - high - middle
    n = a.shape[0]
    out = dot(jnp.concatenate([high, middle, low, jnp.zeros_like(a)], axis=0).astype(BF16), b)
    return out[0:n] + out[n : 2 * n] + out[2 * n : 3 * n]


def one_hot(cond, dtype=BF16):
    return jnp.where(cond, 1.0, 0.0).astype(dtype)


def group_of(lane, z_major):
    return (lane & 31) >> 2 if z_major else lane >> 5


def pack_sums(total, squares, count, z_major):
    row, lane = group_of(iota((256, 128), 0), z_major), iota((256, 128), 1)
    sums = exact(total, one_hot(row == lane)) + exact(squares, one_hot(row == lane - 8))
    sums = jnp.sum(sums, axis=0, keepdims=True)
    at = iota((1, 128), 1)
    return jnp.where(jnp.logical_and(at >= 16, at < 24), count, sums)


def merge(rows):
    counts = jnp.concatenate([rows[:, 16:], rows[:, :16]], axis=1)
    squares = jnp.concatenate([rows[:, 8:], rows[:, :8]], axis=1)
    live = iota(rows.shape, 1) < 8
    counts = jnp.where(live, counts, 1.0)
    total = jnp.sum(rows, axis=0, keepdims=True)
    count = jnp.sum(counts, axis=0, keepdims=True)
    mean = total / count
    off = rows / counts - mean
    spread = jnp.sum(squares + counts * off * off, axis=0, keepdims=True)
    return total, spread, count


def repack(total, spread, count):
    at = iota((1, 128), 1)
    spread = jnp.concatenate([spread[:, 120:], spread[:, :120]], axis=1)
    count = jnp.concatenate([count[:, 112:], count[:, :112]], axis=1)
    tail = jnp.where(at < 24, count, 0.0)
    return jnp.where(at < 8, total, jnp.where(at < 16, spread, tail))


def lanes_of(total, spread, count):
    live = iota((1, 128), 1) < 8
    mean = jnp.where(live, total / count, 0.0)
    scale = jnp.where(live, lax.rsqrt(spread / count + EPS), 0.0)
    both = jnp.concatenate([jnp.broadcast_to(mean, (8, 128)), jnp.broadcast_to(scale, (8, 128))], axis=0)
    wide = exact(both, one_hot(iota((128, 256), 0) == group_of(iota((128, 256), 1), True)))
    return wide[0:1], wide[8:9]


def activated(values, mask, mean, scale, shift):
    half = (values - mean) * (0.5 * scale) + 0.5 * shift
    return jnp.where(mask, half * jnp.tanh(half) + half, 0.0)


def edges(act):
    lane = iota(act.shape, 2)
    before, after = pltpu.roll(act, 1, 1), pltpu.roll(act, 7, 1)
    return jnp.where(lane >= 224, before, jnp.where(lane < 32, after, 0.0))


def kernel(
    n_x, n_y, n_z,
    occ, feat_in, gain_in, shift_in, cw_in, bias_in, qkv_in,
    fine, att,
    feat, gain, shift, cw, bias,
    raw, ends, ends_in, cells, taps, taps_e, mid, taps2, taps2_e, banded, flat,
    weights, qkv_raw, results, tok_f, tok, q_all, k_all, v_all, ready, heads,
    plane_rows, line_rows,
    plane_send, plane_recv, line_send, line_recv, halo_send, halo_recv,
    right_send, right_recv, left_send, left_recv, out_send, out_recv, load_sem,
):
    gx, gy, gz = lax.axis_index("gx"), lax.axis_index("gy"), lax.axis_index("gz")
    n_plane = n_y * n_z
    plane = gy * n_z + gz

    def plane_peer(d):
        other = lax.rem(plane + d, n_plane)
        return (gx, lax.div(other, n_z), lax.rem(other, n_z))

    def line_peer(d):
        return (lax.rem(gx + d, n_x), gy, gz)

    barrier = pltpu.get_barrier_semaphore()

    @pl.loop(1, n_x)
    def _(d):
        pl.semaphore_signal(barrier, inc=1, device_id=line_peer(d), device_id_type=MESH)

    @pl.loop(1, n_plane)
    def _(d):
        pl.semaphore_signal(barrier, inc=1, device_id=plane_peer(d), device_id_type=MESH)

    pairs = (
        (feat_in, feat), (cw_in, cw), (gain_in, gain), (shift_in, shift), (bias_in, bias), (qkv_in, qkv_raw)
    )
    loads = [pltpu.make_async_copy(a, b, load_sem.at[k]) for k, (a, b) in enumerate(pairs)]
    for load in loads:
        load.start()

    def empty(ref):
        ref[...] = jnp.full(ref.shape, EMPTY, BF16)

    pl.when(gx == 0)(lambda: empty(raw.at[0:2, 2:10]))
    pl.when(gx == n_x - 1)(lambda: empty(raw.at[10:12, 2:10]))
    pl.when(gy == 0)(lambda: empty(raw.at[:, 0:2]))
    pl.when(gy == n_y - 1)(lambda: empty(raw.at[:, 10:12]))
    pl.when(gz == 0)(lambda: empty(ends_in.at[0]))
    pl.when(gz == n_z - 1)(lambda: empty(ends_in.at[1]))

    def remote(src, dst, send, recv, peer):
        return pltpu.make_async_remote_copy(
            src_ref=src, dst_ref=dst, send_sem=send, recv_sem=recv, device_id=peer, device_id_type=MESH
        )

    def plane_copy(turn, d):
        return remote(
            plane_rows.at[turn, 0], plane_rows.at[turn, d], plane_send.at[turn, d], plane_recv.at[turn, d], plane_peer(d)
        )

    def line_copy(turn, d):
        return remote(
            line_rows.at[turn, 0], line_rows.at[turn, d], line_send.at[turn, d], line_recv.at[turn, d], line_peer(d)
        )

    def start_all(copy, turn, count):
        @pl.loop(1, count)
        def _(d):
            copy(turn, d).start()

    def wait_recv_all(copy, turn, count):
        @pl.loop(1, count)
        def _(d):
            copy(turn, d).wait_recv()

    def wait_send_all(copy, turn, count):
        @pl.loop(1, count)
        def _(d):
            copy(turn, d).wait_send()

    keeps = [(occ[b, gx] > 0).astype(F32) for b in range(4)]
    brick = iota((8, 4, 256), 1)
    own_keep = jnp.zeros((8, 4, 256), F32)
    for b in range(4):
        own_keep = jnp.where(brick == b, keeps[b], own_keep)
    count = 2048.0 * (keeps[0] + keeps[1] + keeps[2] + keeps[3])
    loads[0].wait()

    def fold(block):
        return jnp.sum(block, axis=0)

    def first_sums(x, acc):
        value = feat[x].astype(F32)
        raw[x + 2, 2:10] = jnp.where(own_keep > 0, value, EMPTY).astype(BF16)
        return acc + fold(value * own_keep)

    total = lax.fori_loop(0, 8, first_sums, jnp.zeros((4, 256), F32))

    def mean_lanes(total, z_major):
        rows = jnp.broadcast_to(jnp.sum(total, axis=0, keepdims=True), (8, 256))
        same = group_of(iota((256, 256), 0), z_major) == group_of(iota((256, 256), 1), z_major)
        return exact(rows, one_hot(same))[0:1] / count

    mean = mean_lanes(total, False)

    def first_squares(x, acc):
        off = (feat[x].astype(F32) - mean) * own_keep
        return acc + fold(off * off)

    squares = lax.fori_loop(0, 8, first_squares, jnp.zeros((4, 256), F32))

    def as_rows(part):
        return jnp.broadcast_to(jnp.sum(part, axis=0, keepdims=True), (8, 256)) * 0.125

    plane_rows[0, 0] = pack_sums(as_rows(total), as_rows(squares), count, False)

    def expand(n):
        flat[:, 0:864] = cw[n].astype(F32)
        whole = flat[...]
        taps_of = [whole[:, 0:128]] + [pltpu.roll(whole, 896 - 96 * t, 1)[:, 0:128] for t in range(1, 9)]
        stacked = jnp.concatenate(taps_of, axis=0).astype(BF16)
        row, lane = iota((128, 256), 0), iota((128, 256), 1)
        same = (row & 31) == (lane & 31)
        for z in range(8):
            here = jnp.logical_and(same, (row >> 5) == (lane >> 5) - z + 1)
            here = jnp.logical_and(here, row < 96)
            moved = dot(stacked, one_hot(here)).astype(BF16)
            banded[n, 0:9, z * 32 : (z + 1) * 32] = moved.reshape(9, 32, 256)
        for z, e, slot in ((0, 0, 7), (7, 2, 0)):
            here = jnp.logical_and(same, jnp.logical_and((row >> 5) == e, (lane >> 5) == slot))
            moved = dot(stacked, one_hot(here)).astype(BF16)
            banded[n, 9:18, z * 32 : (z + 1) * 32] = moved.reshape(9, 32, 256)
        banded[n, 9:18, 32:224] = jnp.zeros((9, 192, 256), BF16)

    flat[:, 768:896] = jnp.zeros((32, 128), F32)

    for load in loads[1:5]:
        load.wait()
    expand(0)
    expand(1)
    spread_lanes = one_hot(iota((32, 256), 0) == (iota((32, 256), 1) & 31))
    small = jnp.concatenate([gain[...], shift[...], bias[...], jnp.zeros((2, 32), F32)], axis=0)
    by_lane = exact(small, spread_lanes)
    pl.semaphore_wait(barrier, n_x + n_plane - 2)
    next_x, last_x = line_peer(1), line_peer(n_x - 1)
    next_y = (gx, lax.rem(gy + 1, n_y), gz)
    last_y = (gx, lax.rem(gy + n_y - 1, n_y), gz)
    next_z = (gx, gy, lax.rem(gz + 1, n_z))
    last_z = (gx, gy, lax.rem(gz + n_z - 1, n_z))

    class Halo:
        def __init__(self, k, index, size, up, down):
            self.has_next, self.has_last = index < size - 1, index > 0
            self.up = remote(up[0], up[1], halo_send.at[k], halo_recv.at[k], up[2])
            self.down = remote(down[0], down[1], halo_send.at[k + 1], halo_recv.at[k + 1], down[2])

        def start(self):
            pl.when(self.has_next)(self.up.start)
            pl.when(self.has_last)(self.down.start)

        def wait_recv(self):
            pl.when(self.has_last)(self.up.wait_recv)
            pl.when(self.has_next)(self.down.wait_recv)

        def wait_send(self):
            pl.when(self.has_next)(self.up.wait_send)
            pl.when(self.has_last)(self.down.wait_send)

    halo_x = Halo(
        0, gx, n_x,
        (raw.at[8:10, 2:10], raw.at[0:2, 2:10], next_x),
        (raw.at[2:4, 2:10], raw.at[10:12, 2:10], last_x),
    )
    halo_y = Halo(
        2, gy, n_y,
        (raw.at[:, 8:10], raw.at[:, 0:2], next_y),
        (raw.at[:, 2:4], raw.at[:, 10:12], last_y),
    )
    halo_z = Halo(
        4, gz, n_z,
        (ends.at[0], ends_in.at[0], next_z),
        (ends.at[1], ends_in.at[1], last_z),
    )
    halo_x.start()
    start_all(plane_copy, 0, n_plane)
    halo_x.wait_recv()
    halo_y.start()
    wait_recv_all(plane_copy, 0, n_plane)
    line_rows[0, 0] = repack(*merge(plane_rows[0].reshape(n_plane, 128)))
    start_all(line_copy, 0, n_x)
    halo_y.wait_recv()

    @pl.loop(0, 12)
    def _(x):
        value = raw[x].astype(F32)
        ends[0, x] = value[:, 3].astype(BF16)
        ends[1, x] = value[:, 0].astype(BF16)
        cells[x, :, 1:5] = value
        cells[x, :, 6:8] = jnp.full((12, 2, 256), EMPTY, F32)

    halo_z.start()
    halo_z.wait_recv()

    lane_in, lane_out = iota((256, 256), 0), iota((256, 256), 1)
    by_z = one_hot(lane_in == ((lane_out & 31) << 3) + (lane_out >> 5))

    @pl.loop(0, 12)
    def _(x):
        cells[x, :, 0] = ends_in[0, x].astype(F32)
        cells[x, :, 5] = ends_in[1, x].astype(F32)
        moved = dot(cells[x].reshape(96, 256).astype(BF16), by_z)
        cells[x] = moved.reshape(12, 8, 256)

    wait_recv_all(line_copy, 0, n_x)
    mean, scale = lanes_of(*merge(line_rows[0].reshape(n_x, 128)))
    scale = scale * by_lane[0:1]

    @pl.loop(0, 12)
    def _(x):
        value = cells[x]
        act = activated(value, value < 512.0, mean, scale, by_lane[2:3])
        edge = edges(act)
        taps[x] = jnp.concatenate([act[0:7], act[5:12]], axis=1).astype(BF16)
        taps_e[x] = jnp.concatenate([edge[0:7], edge[5:12]], axis=1).astype(BF16)

    row8 = iota((1, 8, 256), 1)
    inner = jnp.logical_and(row8 >= 1, row8 < 5)

    @pl.loop(0, 1)
    def _(step):
        x = step * 10
        acc = jnp.zeros((800, 256), F32)
        for tap in range(9):
            dx, dy = tap // 3, tap % 3
            at = pl.ds(x + dx, 10)
            acc = acc + dot(taps[at, dy : dy + 5].reshape(800, 256), banded[0, tap], NT)
            acc = acc + dot(taps_e[at, dy : dy + 5].reshape(800, 256), banded[0, 9 + tap], NT)
        acc = (acc + by_lane[4:5]).reshape(10, 5, 16, 256)
        for k in range(10):
            mid[x + k, 0:5] = jnp.where(cells[x + k + 1, 1:6] < 512.0, acc[k, :, 0:8], 0.0)
            mid[x + k, 5:10] = jnp.where(cells[x + k + 1, 6:11] < 512.0, acc[k, :, 8:16], 0.0)

    def second_sums(x, acc):
        return acc + jnp.sum(jnp.where(inner, mid[x + 1, 1:9], 0.0), axis=0)

    total = lax.fori_loop(0, 8, second_sums, jnp.zeros((8, 256), F32))
    mean = mean_lanes(total, True)

    def second_squares(x, acc):
        keep = jnp.logical_and(inner, cells[x + 2, 2:10] < 512.0)
        off = jnp.where(keep, mid[x + 1, 1:9] - mean, 0.0)
        return acc + jnp.sum(off * off, axis=0)

    squares = lax.fori_loop(0, 8, second_squares, jnp.zeros((8, 256), F32))
    plane_rows[1, 0] = pack_sums(total, squares, count, True)
    start_all(plane_copy, 1, n_plane)
    wait_recv_all(plane_copy, 1, n_plane)
    line_rows[1, 0] = repack(*merge(plane_rows[1].reshape(n_plane, 128)))
    start_all(line_copy, 1, n_x)

    loads[5].wait()
    from_f, to_f = iota((1024, 128), 0), iota((1024, 128), 1)
    source = ((to_f >> 2) << 5) + (to_f & 3)

    @pl.loop(0, 8)
    def _(xy):
        move = one_hot(from_f == source + xy * 4)
        lanes = pl.ds(pl.multiple_of(xy * 128, 128), 128)
        moved = dot(qkv_raw[...].reshape(192, 1024), move)
        for k in range(3):
            weights[k * 128 : k * 128 + 64, lanes] = moved[k * 64 : k * 64 + 64].astype(BF16)
            weights[k * 128 + 64 : k * 128 + 128, lanes] = jnp.zeros((64, 128), BF16)

    wait_recv_all(line_copy, 1, n_x)
    mean, scale = lanes_of(*merge(line_rows[1].reshape(n_x, 128)))
    scale = scale * by_lane[1:2]

    @pl.loop(0, 10)
    def _(x):
        act = activated(mid[x], cells[x + 1, 1:11] < 512.0, mean, scale, by_lane[3:4])
        edge = edges(act)
        taps2[x] = jnp.concatenate([act[0:6], act[4:10]], axis=1).astype(BF16)
        taps2_e[x] = jnp.concatenate([edge[0:6], edge[4:10]], axis=1).astype(BF16)

    wanted = ((((lane_out >> 7) << 2) + (lane_out & 3)) << 5) + ((lane_out & 127) >> 2)
    split = one_hot(lane_in == wanted)
    by_channel = one_hot(lane_in == ((lane_out & 7) << 5) + (lane_out >> 3))
    lower = iota((8, 256), 0) < 4
    steps = n_x // 2
    right, left = line_peer(1), line_peer(n_x - 1)

    def piece(block, c):
        return tok.at[block, pl.ds(c * 16, 16)]

    def go_right(k, c):
        block = lax.rem(gx - k + n_x, n_x)
        return remote(piece(block, c), piece(block, c), right_send.at[k, c], right_recv.at[k, c], right)

    def go_left(k, c):
        block = lax.rem(gx + k, n_x)
        return remote(piece(block, c), piece(block, c), left_send.at[k, c], left_recv.at[k, c], left)

    @pl.loop(0, 2)
    def _(step):
        x = step * 4
        acc = jnp.zeros((256, 256), F32)
        for tap in range(9):
            dx, dy = tap // 3, tap % 3
            at = pl.ds(x + dx, 4)
            acc = acc + dot(taps2[at, dy : dy + 4].reshape(256, 256), banded[1, tap], NT)
            acc = acc + dot(taps2_e[at, dy : dy + 4].reshape(256, 256), banded[1, 9 + tap], NT)
        acc = (acc + by_lane[5:6]).reshape(4, 4, 16, 256)
        rows = []
        for k in range(4):
            value = jnp.concatenate([cells[x + k + 2, 2:6], cells[x + k + 2, 6:10]], axis=1)
            result = jnp.where(value < 512.0, value + acc[k], 0.0)
            rows.append(result.astype(BF16).reshape(64, 256))
        rows = jnp.concatenate(rows, axis=0)
        moved = dot(rows, split).reshape(4, 4, 16, 256)
        for half in range(2):
            for k in range(2):
                for y in range(4):
                    low, high = moved[2 * half + k, y, 0:8], moved[2 * half + k, y, 8:16]
                    tile = jnp.where(lower, pltpu.roll(low, 7, 0), pltpu.roll(high, 3, 0))
                    lanes = slice((k * 4 + y) * 128, (k * 4 + y + 1) * 128)
                    tok_f[half, 0:8, lanes] = tile[:, 0:128]
                    tok_f[half, 8:16, lanes] = tile[:, 128:256]
            c = step * 2 + half
            tok[gx, pl.ds(pl.multiple_of(c * 16, 16), 16)] = tok_f[half].astype(BF16)
            go_right(0, c).start()
            go_left(0, c).start()
        results[step] = rows

    lane = iota((64, 128), 1)
    brick_row = iota((64, 128), 0) & 3

    def project(blocks):
        together = jnp.concatenate([tok[block] for block in blocks], axis=0)
        outs = dot(together, weights[...], NT)
        for j, block in enumerate(blocks):
            out = outs[j * 64 : (j + 1) * 64]
            at = pl.ds(pl.multiple_of(block * 64, 64), 64)
            far = jnp.zeros((64, 128), F32)
            for b in range(4):
                keep = (occ[b, block] > 0).astype(F32)
                far = jnp.where(brick_row == b, (1.0 - keep) * FAR, far)
            q_all[at] = jnp.where(lane == 64, 1.0, out[:, 0:128].astype(BF16).astype(F32) * 0.125).astype(BF16)
            k_all[at] = jnp.where(lane == 64, far, out[:, 128:256]).astype(BF16)
            v_all[at] = jnp.where(lane == 64, 1.0, out[:, 256:384]).astype(BF16)

    project([gx])

    @pl.loop(0, 2)
    def _(step):
        moved = dot(results[step], by_channel).reshape(4, 4, 16, 256)
        for k in range(4):
            fine[step * 4 + k, 0:4] = moved[k, :, 1:5].astype(BF16)
            fine[step * 4 + k, 4:8] = moved[k, :, 9:13].astype(BF16)

    @pl.loop(1, steps)
    def _(k):
        more = k < steps - 1
        for c in range(PIECES):
            go_right(k - 1, c).wait_recv()
            pl.when(jnp.logical_or(more, c < PIECES // 2))(go_right(k, c).start)
            go_left(k - 1, c).wait_recv()
            pl.when(jnp.logical_or(more, c >= PIECES // 2))(go_left(k, c).start)
        project([lax.rem(gx - k + n_x, n_x), lax.rem(gx + k, n_x)])

    for c in range(PIECES):
        if c < PIECES // 2:
            go_right(steps - 1, c).wait_recv()
        else:
            go_left(steps - 1, c).wait_recv()
    project([lax.rem(gx + steps, n_x)])

    def attend(members):
        at = [pl.ds(pl.multiple_of(m * 64, 64), 64) for m in members]
        queries = jnp.concatenate([q_all[a] for a in at], axis=0)
        scores = dot(queries, k_all[...], NT)
        probs = jnp.exp(scores - jnp.max(scores, axis=1, keepdims=True))
        mixed = dot(probs.astype(BF16), v_all[...])
        result = mixed / mixed[:, 64:65]
        low = iota((32, 128), 1) < 64
        for j, m in enumerate(members):
            top, bottom = result[64 * j : 64 * j + 32], result[64 * j + 32 : 64 * j + 64]
            ready[m] = jnp.where(low, top, pltpu.roll(bottom, 64, 1)).astype(BF16)

    def out_copy(d):
        m = lax.rem(gx + d, n_x)
        return remote(ready.at[m], heads.at[gx], out_send.at[d], out_recv.at[gx], line_peer(d))

    @pl.loop(0, n_x // 4)
    def _(k):
        ahead = (steps + 2 * k, steps + 2 * k + 1, steps - 1 - 2 * k, steps - 2 - 2 * k)
        attend([lax.rem(gx + d, n_x) for d in ahead])
        for d in ahead[0:3]:
            out_copy(d).start()
        pl.when(ahead[3] > 0)(out_copy(ahead[3]).start)

    heads[gx] = ready[gx]

    @pl.loop(1, n_x)
    def _(d):
        m = lax.rem(gx + d, n_x)
        remote(ready.at[m], heads.at[m], out_send.at[d], out_recv.at[m], line_peer(d)).wait_recv()

    low = iota((32, 128), 1) < 64
    tops, bottoms = [], []
    for t in range(n_x // 2):
        even, odd = heads[2 * t].astype(F32), heads[2 * t + 1].astype(F32)
        tops.append(jnp.where(low, even, pltpu.roll(odd, 64, 1)))
        bottoms.append(jnp.where(low, pltpu.roll(even, 64, 1), odd))
    stacked = jnp.concatenate([jnp.concatenate(tops, axis=1), jnp.concatenate(bottoms, axis=1)], axis=0)
    row, col = iota((64, 64), 0), iota((64, 64), 1)
    source = ((row >> 4) << 4) + ((row & 1) << 3) + (((row & 15) >> 3) << 2) + ((row & 7) >> 1)
    order = one_hot(source == col)
    placed = dot(order, stacked.astype(BF16))
    row = (iota(placed.shape, 0) >> 1) & 3
    keep_rows = jnp.zeros(placed.shape, F32)
    for b in range(4):
        keep_rows = jnp.where(row == b, keeps[b], keep_rows)
    att[...] = (placed * keep_rows).astype(BF16)

    for turn in range(2):
        wait_send_all(plane_copy, turn, n_plane)
        wait_send_all(line_copy, turn, n_x)
    for halo in (halo_x, halo_y, halo_z):
        halo.wait_send()

    @pl.loop(0, steps - 1)
    def _(k):
        for c in range(PIECES):
            go_right(k, c).wait_send()
            go_left(k, c).wait_send()

    for c in range(PIECES):
        if c < PIECES // 2:
            go_right(steps - 1, c).wait_send()
        else:
            go_left(steps - 1, c).wait_send()

    @pl.loop(1, n_x)
    def _(d):
        out_copy(d).wait_send()


def body(n_x, n_y, n_z, features, occupancy, norm_gain, norm_shift, conv_weight, conv_bias, qkv_weight):
    vmem = pl.BlockSpec(memory_space=pltpu.VMEM)
    smem = pl.BlockSpec(memory_space=pltpu.SMEM)
    hbm = pl.BlockSpec(memory_space=pltpu.HBM)
    dma = pltpu.SemaphoreType.DMA
    n_plane = n_y * n_z
    half = n_x // 2
    fine, att = pl.pallas_call(
        functools.partial(kernel, n_x, n_y, n_z),
        out_shape=(
            jax.ShapeDtypeStruct((8, 8, 4, 256), BF16),
            jax.ShapeDtypeStruct((64, 1024), BF16),
        ),
        in_specs=[smem] + [hbm] * 6,
        out_specs=(vmem, vmem),
        scratch_shapes=[
            pltpu.VMEM((8, 8, 4, 256), BF16),
            pltpu.VMEM((2, 32), F32),
            pltpu.VMEM((2, 32), F32),
            pltpu.VMEM((2, 32, 864), BF16),
            pltpu.VMEM((2, 32), F32),
            pltpu.VMEM((12, 12, 4, 256), BF16),
            pltpu.VMEM((2, 12, 12, 256), BF16),
            pltpu.VMEM((2, 12, 12, 256), BF16),
            pltpu.VMEM((12, 12, 8, 256), F32),
            pltpu.VMEM((12, 7, 16, 256), BF16),
            pltpu.VMEM((12, 7, 16, 256), BF16),
            pltpu.VMEM((10, 10, 8, 256), F32),
            pltpu.VMEM((10, 6, 16, 256), BF16),
            pltpu.VMEM((10, 6, 16, 256), BF16),
            pltpu.VMEM((2, 18, 256, 256), BF16),
            pltpu.VMEM((32, 896), F32),
            pltpu.VMEM((384, 1024), BF16),
            pltpu.VMEM((3, 64, 1024), BF16),
            pltpu.VMEM((2, 256, 256), BF16),
            pltpu.VMEM((2, 16, 1024), F32),
            pltpu.VMEM((n_x, 64, 1024), BF16),
            pltpu.VMEM((n_x * 64, 128), BF16),
            pltpu.VMEM((n_x * 64, 128), BF16),
            pltpu.VMEM((n_x * 64, 128), BF16),
            pltpu.VMEM((n_x, 32, 128), BF16),
            pltpu.VMEM((n_x, 32, 128), BF16),
            pltpu.VMEM((2, n_plane, 1, 128), F32),
            pltpu.VMEM((2, n_x, 1, 128), F32),
            dma((2, n_plane)), dma((2, n_plane)), dma((2, n_x)), dma((2, n_x)),
            dma((6,)), dma((6,)),
            dma((half, PIECES)), dma((half, PIECES)), dma((half, PIECES)), dma((half, PIECES)),
            dma((n_x,)), dma((n_x,)), dma((6,)),
        ],
        compiler_params=pltpu.CompilerParams(
            collective_id=0, has_side_effects=True, vmem_limit_bytes=50 * 1024 * 1024
        ),
    )(
        *[
            pltpu.with_memory_space_constraint(a, pltpu.HBM)
            for a in (
                jnp.transpose(occupancy, (1, 2, 0))[0],
                features, norm_gain, norm_shift, conv_weight, conv_bias, qkv_weight,
            )
        ]
    )
    return fine, att[None]


def solution(mesh):
    in_specs = (P("gx", "gy", "gz", None), P(None, "gy", "gz"), P(), P(), P(), P(), P(None, "gx", None))
    out_specs = (P("gx", "gy", "gz", None), P(("gy", "gz"), "gx", None))
    sizes = tuple(mesh.shape[a] for a in ("gx", "gy", "gz"))
    return jax.shard_map(
        functools.partial(body, *sizes), mesh=mesh, in_specs=in_specs, out_specs=out_specs, check_vma=False
    )
```
